512 devices in a mesh: tm: 8 (over x, core), dp: 64 (over z, y).
Axes of the slice: x: 4, y: 4, z: 16, core: 2. Of those that a mesh axis runs over, the one named last changes fastest.
Arguments:
- edge_feat: bfloat16 [8, 8192, 186], P('tm', 'dp'), may hold values from -6 to 6
- endpoint_slots: int32 [8, 2, 8192], P('tm', None, 'dp'), may hold values from 0 to 2047, as said below
- neighbor_slots: int32 [8, 20, 8192], P('tm', None, 'dp'), may hold values from 0 to 2047, as said below
- neighbor_gap: int32 [8, 20, 8192], P('tm', None, 'dp'), may hold values from 0 to 999
- score_grad: float32 [8, 8192], P('tm', 'dp'), may hold values from -1.5 to 1.5
- node_list: int32 [8, 64, 2048], P('tm', 'dp'), may hold values from 0 to 128, as said below
- memory0: float32 [8192, 256], P('dp'), may hold values from -6 to 6
- msg_weight: bfloat16 [186, 256], replicated, may hold values from -0.4375 to 0.4375
- gate_weight: bfloat16 [256, 512], replicated, may hold values from -0.375 to 0.375
- gate_bias: float32 [512], replicated, may hold values from -4 to 4
- omega: float32 [256], replicated, may hold values from 0.001 to 1
- attn_weights: bfloat16 [4, 256, 256], replicated, may hold values from -0.375 to 0.375
- pred_weights: bfloat16 [2, 256, 256], replicated, may hold values from -0.375 to 0.375
- pred_out: float32 [256], replicated, may hold values from -0.375 to 0.375
Outputs:
- scores: float32 [8, 8192], P('tm', 'dp')
- new_memory: float32 [8, 8192, 256], P('tm', 'dp')
- grad_out_proj: float32 [256, 256], replicated
- grad_pred: float32 [2, 256, 256], replicated
The draws below stay inside these ranges and needn't reach their ends.
Inputs may be any that keep to these rules, and one draw needn't show every extreme that they name: `node_list`: each block of 32 slots (one device's requests to one owner) holds distinct rows first and 128 in the empty slots after them; every block holds at least one row; in each mini-batch some owner's block is full from every device. `endpoint_slots`: every slot points at a non-empty entry of its device's node list. `neighbor_slots`: every slot points at a non-empty entry of its device's node list.
All inputs are finite; a program needn't handle non-finite values.
Results may differ from the reference program's by a relative error of at most 0.017.
Values may be sent and summed in bfloat16 or wider, within the bound.
No kernel may reach another device: no remote copies, remote signals or barrier semaphores. Data moves between devices by JAX's collectives and lax.ppermute only.
A program may use at most 64 MiB of HBM per device.

```python
import math
import jax
import jax.numpy as jnp
from jax import lax

DM = 256
HEADS = 2
EF = 186
NBRS = 10
NODE_DEV = 128
EVT_DEV = 128
LIST = 2048
CAP = 32
NODES = 8192
EVENTS = 8192
N_TM = 8
N_DP = 64


def slot_counts(key):
    salted = jax.random.fold_in(key, 101)
    hot_owner = jax.random.randint(jax.random.fold_in(salted, 1), (N_TM,), 0, N_DP)
    least = max(CAP // 4, 1)
    counts = jax.random.randint(jax.random.fold_in(salted, 2), (N_TM, N_DP, N_DP), least, CAP + 1)
    owners = jnp.arange(N_DP)
    return jnp.where(owners[None, None, :] == hot_owner[:, None, None], CAP, counts)


def pick_slots(key, row_count, salt):
    counts = slot_counts(key)
    salted = jax.random.fold_in(key, salt)
    owner_of = jax.random.randint(jax.random.fold_in(salted, 1), (N_TM, row_count, EVENTS), 0, N_DP)
    device_of = jnp.arange(EVENTS) // EVT_DEV
    limit_of = counts[jnp.arange(N_TM)[:, None, None], device_of[None, None, :], owner_of]
    position = jax.random.randint(jax.random.fold_in(salted, 2), (N_TM, row_count, EVENTS), 0, limit_of)
    return (owner_of * CAP + position).astype(jnp.int32)


def draw_node_list(key, part):
    counts = slot_counts(key)
    subkeys = jax.random.split(jax.random.fold_in(key, 102), N_TM * N_DP * N_DP)
    chosen = jax.vmap(lambda subkey: jax.random.permutation(subkey, NODE_DEV)[:CAP])(subkeys)
    chosen = chosen.reshape(N_TM, N_DP, N_DP, CAP)
    filled = jnp.arange(CAP)[None, None, None, :] < counts[..., None]
    return jnp.where(filled, chosen, NODE_DEV).reshape(N_TM, N_DP, LIST).astype(jnp.int32)


def draw_endpoint_slots(key, part):
    return pick_slots(key, 2, 103)


def draw_neighbor_slots(key, part):
    return pick_slots(key, 2 * NBRS, 104)


def with_ends(values, rng, low, largest):
    shape = values.shape
    spot = [jax.random.randint(jax.random.fold_in(rng, axis), (), 0, shape[axis]) for axis in range(len(shape))]
    values = values.at[tuple(spot)].set(low)
    longest = shape.index(max(shape))
    spot[longest] = (spot[longest] + 1) % shape[longest]
    return values.at[tuple(spot)].set(largest)


def level_of(rng, shape, cuts, low, top_value):
    def one(dim, parts):
        draws = jax.random.uniform(jax.random.fold_in(jax.random.fold_in(rng, 6), dim), (parts,), jnp.float32, low / len(cuts), top_value / len(cuts))
        return jnp.repeat(jnp.exp(draws), shape[dim] // parts).reshape((-1,) + (1,) * (len(shape) - dim - 1))

    factor_of = one(*cuts[0])
    for cut in cuts[1:]:
        factor_of = factor_of * one(*cut)
    return factor_of


def scatter_about(own_key, dims, deviation, limit, cuts=(), kind=jnp.bfloat16):
    gain = level_of(own_key, dims, cuts, -0.22, 0.18) if cuts else 1.0
    values = jax.random.normal(own_key, dims, jnp.float32) * deviation * gain
    return jnp.minimum(jnp.maximum(values, -limit), limit).astype(kind)


def setup_inputs(seed: int = 0) -> dict:
    seeds = jax.random.split(jax.random.key(seed), 15)
    edge_feat = scatter_about(seeds[0], (N_TM, EVENTS, EF), 1.0, 6.0, ((0, 8), (1, 64)))
    endpoint_slots = draw_endpoint_slots(jax.random.fold_in(seeds[14], 71), 0)
    neighbor_slots = draw_neighbor_slots(jax.random.fold_in(seeds[14], 71), 0)
    neighbor_gap = with_ends(jax.random.randint(seeds[3], (N_TM, 2 * NBRS, EVENTS), 0, 1000), jax.random.fold_in(seeds[3], 1), 0, 999).astype(jnp.int32)
    score_grad = scatter_about(seeds[4], (N_TM, EVENTS), 0.25, 1.5, ((0, 8), (1, 64)), jnp.float32)
    node_list = draw_node_list(jax.random.fold_in(seeds[14], 71), 0)
    memory0 = scatter_about(seeds[6], (NODES, DM), 1.0, 6.0, ((0, 64),), jnp.float32)
    msg_weight = scatter_about(seeds[7], (EF, DM), EF ** -0.5, 0.4375)
    gate_weight = scatter_about(seeds[8], (DM, 2 * DM), DM ** -0.5, 0.375)
    gate_bias = scatter_about(seeds[9], (2 * DM,), 1.0, 4.0, (), jnp.float32)
    omega = jnp.clip(jnp.exp(jax.random.uniform(seeds[10], (DM,), jnp.float32, math.log(0.001), math.log(1.0))), 0.001, 1.0)
    attn_weights = scatter_about(seeds[11], (4, DM, DM), DM ** -0.5, 0.375)
    pred_weights = scatter_about(seeds[12], (2, DM, DM), DM ** -0.5, 0.375)
    pred_out = scatter_about(seeds[13], (DM,), DM ** -0.5, 0.375, (), jnp.float32)
    return {"edge_feat": edge_feat, "endpoint_slots": endpoint_slots, "neighbor_slots": neighbor_slots, "neighbor_gap": neighbor_gap, "score_grad": score_grad, "node_list": node_list, "memory0": memory0, "msg_weight": msg_weight, "gate_weight": gate_weight, "gate_bias": gate_bias, "omega": omega, "attn_weights": attn_weights, "pred_weights": pred_weights, "pred_out": pred_out}


def local_step(slot_rows, end_slots, near_slots, near_gaps, cot_rows, omega, attn_weights, pred_weights, pred_out):
    feat_width = slot_rows.shape[1]
    events = end_slots.shape[1]
    near_count = near_slots.shape[0] // 2
    head_dim = feat_width // HEADS
    self_rows = jnp.take(slot_rows, end_slots, axis=0)
    near_rows = jnp.take(slot_rows, near_slots, axis=0).reshape(2, near_count, events, feat_width)
    phases = near_gaps.reshape(2, near_count, events).astype(jnp.float32)[..., None] * omega
    near_feat = (near_rows.astype(jnp.float32) + jnp.cos(phases)).astype(jnp.bfloat16)
    query_proj = jnp.einsum('pea,ab->peb', self_rows, attn_weights[0], preferred_element_type=jnp.float32)
    key_proj = jnp.einsum('pkea,ab->pkeb', near_feat, attn_weights[1], preferred_element_type=jnp.float32)
    value_proj = jnp.einsum('pkea,ab->pkeb', near_feat, attn_weights[2], preferred_element_type=jnp.float32)
    query_heads = query_proj.reshape(2, 1, events, HEADS, head_dim)
    key_heads = key_proj.reshape(2, near_count, events, HEADS, head_dim)
    value_heads = value_proj.reshape(2, near_count, events, HEADS, head_dim)
    att_logits = lax.optimization_barrier(jnp.sum(query_heads * key_heads, axis=-1)) / math.sqrt(head_dim)
    weights_att = jax.nn.softmax(att_logits, axis=1)
    mixed_heads = lax.optimization_barrier(jnp.sum(weights_att[..., None] * value_heads, axis=1)).reshape(2, events, feat_width).astype(jnp.bfloat16)
    state_full = self_rows.astype(jnp.float32) + jnp.einsum('pea,ab->peb', mixed_heads, attn_weights[3], preferred_element_type=jnp.float32)
    state_bf = state_full.astype(jnp.bfloat16)
    pre_pred = jnp.dot(state_bf[0], pred_weights[0], preferred_element_type=jnp.float32) + jnp.dot(state_bf[1], pred_weights[1], preferred_element_type=jnp.float32)
    sigmoid_pre = jax.nn.sigmoid(pre_pred)
    logit_out = lax.optimization_barrier(jnp.sum(pre_pred * sigmoid_pre * pred_out, axis=-1))
    grad_pre = (cot_rows[:, None] * pred_out * (sigmoid_pre * (1.0 + pre_pred * (1.0 - sigmoid_pre)))).astype(jnp.bfloat16)
    grad_first = jnp.einsum('ea,eb->ab', state_bf[0], grad_pre, preferred_element_type=jnp.float32)
    grad_second = jnp.einsum('ea,eb->ab', state_bf[1], grad_pre, preferred_element_type=jnp.float32)
    grad_state = jnp.einsum('eb,pab->pea', grad_pre, pred_weights, preferred_element_type=jnp.float32).astype(jnp.bfloat16)
    grad_out_proj = jnp.einsum('pea,peb->ab', mixed_heads, grad_state, preferred_element_type=jnp.float32)
    return (logit_out, grad_out_proj, jnp.stack([grad_first, grad_second]))

def reference(edge_feat, endpoint_slots, neighbor_slots, neighbor_gap, score_grad, node_list, memory0, msg_weight, gate_weight, gate_bias, omega, attn_weights, pred_weights, pred_out):
    owner_of = (jnp.arange(LIST) // CAP).astype(jnp.int32)
    node_rows = jnp.where(node_list < NODE_DEV, owner_of * NODE_DEV + node_list, NODES).astype(jnp.int32)
    device_of = (jnp.arange(EVENTS) // EVT_DEV).astype(jnp.int32)
    memory = memory0
    logit_list = []
    memory_list = []
    grad_out = jnp.zeros((DM, DM), jnp.float32)
    grad_pair = jnp.zeros((2, DM, DM), jnp.float32)
    for batch_index in range(N_TM):
        row_table = node_rows[batch_index]
        end_slots = endpoint_slots[batch_index]
        end_rows = row_table[device_of[None, :], end_slots].reshape(-1)
        message = jnp.dot(edge_feat[batch_index], msg_weight, preferred_element_type=jnp.float32).astype(jnp.bfloat16)
        message = lax.optimization_barrier(message).astype(jnp.float32)
        slot_sums = jax.ops.segment_sum(jnp.concatenate([message, message]), end_rows, NODES + 1)[:NODES]
        counts = jax.ops.segment_sum(jnp.ones((2 * EVENTS,), jnp.float32), end_rows, NODES + 1)[:NODES]
        touched = (counts > 0.5).astype(jnp.float32)
        mean_msg = (slot_sums / jnp.maximum(counts, 1.0)[:, None]).astype(jnp.bfloat16)
        pre_gate = jnp.dot(mean_msg, gate_weight, preferred_element_type=jnp.float32) + gate_bias
        update = jax.nn.sigmoid(pre_gate[:, :DM]) * touched[:, None]
        candidate = jnp.tanh(pre_gate[:, DM:])
        decay_rate = 1.0 - update
        inject = update * candidate
        padded = jnp.concatenate([memory.astype(jnp.bfloat16), jnp.zeros((1, DM), jnp.bfloat16)])
        slot_rows = jnp.take(padded, row_table, axis=0)
        ends_dev = end_slots.reshape(2, N_DP, EVT_DEV).transpose(1, 0, 2)
        near_dev = neighbor_slots[batch_index].reshape(2 * NBRS, N_DP, EVT_DEV).transpose(1, 0, 2)
        gaps_dev = neighbor_gap[batch_index].reshape(2 * NBRS, N_DP, EVT_DEV).transpose(1, 0, 2)
        cot_dev = score_grad[batch_index].reshape(N_DP, EVT_DEV)

        def per_device(packed):
            return local_step(packed[0], packed[1], packed[2], packed[3], packed[4], omega, attn_weights, pred_weights, pred_out)
        logit_out, grad_o, grad_p = lax.map(per_device, (slot_rows, ends_dev, near_dev, gaps_dev, cot_dev))
        grad_out = grad_out + lax.optimization_barrier(jnp.sum(grad_o, axis=0))
        grad_pair = grad_pair + lax.optimization_barrier(jnp.sum(grad_p, axis=0))
        logit_list.append(logit_out.reshape(EVENTS))
        memory = decay_rate * memory + inject
        memory_list.append(memory)
    return (jnp.stack(logit_list), jnp.stack(memory_list), grad_out, grad_pair)
```

```python
import math

import jax
import jax.numpy as jnp
from jax import lax
from jax.sharding import PartitionSpec as P

HEADS = 2


def local_step(
    slot_rows,
    end_slots,
    near_slots,
    near_gaps,
    cot_rows,
    omega,
    attn_weights,
    pred_weights,
    pred_out,
):
    feat_width = slot_rows.shape[1]
    events = end_slots.shape[1]
    near_count = near_slots.shape[0] // 2
    head_dim = feat_width // HEADS
    self_rows = jnp.take(slot_rows, end_slots, axis=0)
    near_rows = jnp.take(slot_rows, near_slots, axis=0).reshape(2, near_count, events, feat_width)
    phases = near_gaps.reshape(2, near_count, events).astype(jnp.float32)[..., None] * omega
    near_feat = (near_rows.astype(jnp.float32) + jnp.cos(phases)).astype(jnp.bfloat16)
    query_proj = jnp.einsum(
        "pea,ab->peb", self_rows, attn_weights[0], preferred_element_type=jnp.float32
    )
    key_proj = jnp.einsum(
        "pkea,ab->pkeb", near_feat, attn_weights[1], preferred_element_type=jnp.float32
    )
    value_proj = jnp.einsum(
        "pkea,ab->pkeb", near_feat, attn_weights[2], preferred_element_type=jnp.float32
    )
    query_heads = query_proj.reshape(2, 1, events, HEADS, head_dim)
    key_heads = key_proj.reshape(2, near_count, events, HEADS, head_dim)
    value_heads = value_proj.reshape(2, near_count, events, HEADS, head_dim)
    att_logits = jnp.sum(query_heads * key_heads, axis=-1) / math.sqrt(head_dim)
    weights_att = jax.nn.softmax(att_logits, axis=1)
    mixed_heads = (
        jnp.sum(weights_att[..., None] * value_heads, axis=1)
        .reshape(2, events, feat_width)
        .astype(jnp.bfloat16)
    )
    state_full = self_rows.astype(jnp.float32) + jnp.einsum(
        "pea,ab->peb", mixed_heads, attn_weights[3], preferred_element_type=jnp.float32
    )
    state_bf = state_full.astype(jnp.bfloat16)
    pre_pred = jnp.dot(state_bf[0], pred_weights[0], preferred_element_type=jnp.float32) + jnp.dot(
        state_bf[1], pred_weights[1], preferred_element_type=jnp.float32
    )
    sigmoid_pre = jax.nn.sigmoid(pre_pred)
    logit_out = jnp.sum(pre_pred * sigmoid_pre * pred_out, axis=-1)
    grad_pre = (
        cot_rows[:, None] * pred_out * (sigmoid_pre * (1.0 + pre_pred * (1.0 - sigmoid_pre)))
    ).astype(jnp.bfloat16)
    grad_first = jnp.einsum("ea,eb->ab", state_bf[0], grad_pre, preferred_element_type=jnp.float32)
    grad_second = jnp.einsum("ea,eb->ab", state_bf[1], grad_pre, preferred_element_type=jnp.float32)
    grad_state = jnp.einsum(
        "eb,pab->pea", grad_pre, pred_weights, preferred_element_type=jnp.float32
    ).astype(jnp.bfloat16)
    grad_out_proj = jnp.einsum(
        "pea,peb->ab", mixed_heads, grad_state, preferred_element_type=jnp.float32
    )
    return (logit_out, grad_out_proj, jnp.stack([grad_first, grad_second]))


def exchange(value, axis):
    return lax.all_to_all(value, axis, split_axis=0, concat_axis=0, tiled=True)


def sum_everywhere(grads):
    parts, spots = lax.axis_size("tm"), lax.axis_size("dp")
    rows, width = grads.shape
    own = rows // parts
    pieces = exchange(grads.astype(jnp.bfloat16).reshape(parts, own, width), "tm")
    mine = jnp.sum(pieces.astype(jnp.float32), axis=0).astype(jnp.bfloat16)
    cells = own * width // spots // 128
    pieces = exchange(mine.reshape(spots, cells, 128), "dp")
    mine = jnp.sum(pieces.astype(jnp.float32), axis=0).astype(jnp.bfloat16)
    whole = exchange(jnp.broadcast_to(mine[None], (spots, cells, 128)), "dp")
    whole = whole.reshape(own, width)
    return lax.all_gather(whole, "tm", axis=0, tiled=True).astype(jnp.float32)


def per_device(
    edge_feat,
    endpoint_slots,
    neighbor_slots,
    neighbor_gap,
    score_grad,
    node_list,
    memory0,
    msg_weight,
    gate_weight,
    gate_bias,
    omega,
    attn_weights,
    pred_weights,
    pred_out,
):
    groups = lax.axis_size("dp")
    batches = lax.axis_size("tm")
    node_dev, feat_width = memory0.shape
    list_len = node_list.shape[2]
    per_owner = list_len // groups
    requests = node_list[0, 0].reshape(groups, per_owner)
    message = jnp.dot(edge_feat[0], msg_weight, preferred_element_type=jnp.float32).astype(
        jnp.bfloat16
    )
    end_slots = endpoint_slots[0]
    slot_of = jnp.arange(list_len, dtype=jnp.int32)[:, None]
    hits = (end_slots[0][None, :] == slot_of).astype(jnp.float32) + (
        end_slots[1][None, :] == slot_of
    ).astype(jnp.float32)
    slot_tally = jnp.sum(hits, axis=1).astype(jnp.int32)
    slot_sums = jnp.dot(
        hits.astype(jnp.bfloat16), message, preferred_element_type=jnp.float32
    ).astype(jnp.bfloat16)
    small = exchange(
        jnp.concatenate([requests, slot_tally.reshape(groups, per_owner)], axis=1), "dp"
    )
    got_sums = exchange(slot_sums.reshape(groups, per_owner, feat_width), "dp")
    wanted = small[:, :per_owner].reshape(-1)
    got_tally = small[:, per_owner:].reshape(-1)
    picker = (wanted[:, None] == jnp.arange(node_dev)[None, :]).astype(jnp.bfloat16)
    totals = jnp.einsum(
        "sn,sd->nd", picker, got_sums.reshape(-1, feat_width), preferred_element_type=jnp.float32
    )
    counts = jnp.sum(
        jnp.where(wanted[:, None] == jnp.arange(node_dev)[None, :], got_tally[:, None], 0), axis=0
    ).astype(jnp.float32)
    touched = (counts > 0.5).astype(jnp.float32)
    mean_msg = (totals / jnp.maximum(counts, 1.0)[:, None]).astype(jnp.bfloat16)
    pre_gate = jnp.dot(mean_msg, gate_weight, preferred_element_type=jnp.float32) + gate_bias
    update = jax.nn.sigmoid(pre_gate[:, :feat_width]) * touched[:, None]
    candidate = jnp.tanh(pre_gate[:, feat_width:])
    decay_rate = 1.0 - update
    inject = update * candidate
    section_index = lax.axis_index("tm")
    share = node_dev // batches
    steps = exchange(
        jnp.concatenate(
            [
                decay_rate.astype(jnp.bfloat16).reshape(batches, share, feat_width),
                inject.astype(jnp.bfloat16).reshape(batches, share, feat_width),
            ],
            axis=1,
        ),
        "tm",
    ).astype(jnp.float32)
    state = lax.dynamic_slice_in_dim(memory0, section_index * share, share, axis=0)
    states = []
    for batch in range(batches):
        states.append(state.astype(jnp.bfloat16))
        state = steps[batch, :share] * state + steps[batch, share:]
    memory_bf = exchange(jnp.stack(states), "tm").reshape(node_dev, feat_width)
    before = jnp.where(section_index == 0, memory0, memory_bf.astype(jnp.float32))
    new_memory = decay_rate * before + inject
    sent_rows = jnp.dot(picker, memory_bf, preferred_element_type=jnp.float32).astype(jnp.bfloat16)
    slot_rows = exchange(sent_rows.reshape(groups, per_owner, feat_width), "dp").reshape(
        list_len, feat_width
    )
    logit_out, grad_out, grad_pair = local_step(
        slot_rows,
        end_slots,
        neighbor_slots[0],
        neighbor_gap[0],
        score_grad[0],
        omega,
        attn_weights,
        pred_weights,
        pred_out,
    )
    grads = sum_everywhere(jnp.concatenate([grad_out[None], grad_pair]).reshape(-1, feat_width))
    grads = grads.reshape(3, feat_width, feat_width)
    return (logit_out[None, :], new_memory[None], grads[0], grads[1:])


def solution(mesh):
    in_specs = (
        P("tm", "dp", None),
        P("tm", None, "dp"),
        P("tm", None, "dp"),
        P("tm", None, "dp"),
        P("tm", "dp"),
        P("tm", "dp", None),
        P("dp", None),
        P(),
        P(),
        P(),
        P(),
        P(),
        P(),
        P(),
    )
    out_specs = (P("tm", "dp"), P("tm", "dp", None), P(), P())
    return jax.shard_map(
        per_device, mesh=mesh, in_specs=in_specs, out_specs=out_specs, check_vma=False
    )
```

```python
import math

import jax
import jax.numpy as jnp
from jax import lax
from jax.experimental import pallas as pl
from jax.experimental.pallas import tpu as pltpu
from jax.sharding import PartitionSpec as P

HEADS = 2
LANES = 128
HALF = LANES // 2
NT = (((1,), (1,)), ((), ()))
TN = (((0,), (0,)), ((), ()))
F32 = jnp.float32
BF16 = jnp.bfloat16
PARAMS = pltpu.CompilerParams(vmem_limit_bytes=40 * 1024 * 1024)


def lane_index(shape):
    return lax.broadcasted_iota(jnp.int32, shape, len(shape) - 1)


def dot(left, right, dims=(((1,), (0,)), ((), ()))):
    return lax.dot_general(left, right, dims, preferred_element_type=F32)


def dense_call(body, out_shape, args, scratch=()):
    return pl.pallas_call(
        body,
        out_shape=out_shape,
        in_specs=[pl.BlockSpec(memory_space=pltpu.VMEM)] * len(args),
        scratch_shapes=list(scratch),
        compiler_params=PARAMS,
    )(*args)


def pack_body(feat_ref, ends_ref, list_ref, out_ref, wide_ref):
    rest = feat_ref.shape[0] - LANES
    wide_ref[...] = jnp.zeros_like(wide_ref)
    wide_ref[0:rest, :] = feat_ref[LANES:, :].astype(F32)
    tail = wide_ref[...].astype(BF16)
    empty = jnp.zeros_like(tail)
    tails = jnp.concatenate(
        [
            jnp.concatenate([tail, empty], axis=0),
            jnp.concatenate([empty, tail], axis=0),
        ],
        axis=1,
    )
    head = feat_ref[0:LANES, :]
    per_owner = out_ref.shape[1] * 2 // 3
    low = per_owner // 2
    owners = LANES // per_owner
    slot_of = lax.broadcasted_iota(jnp.int32, (LANES, LANES), 0)
    diagonal = slot_of == lane_index((LANES, LANES))
    ends = ends_ref[...]
    lane = lane_index((1, 1, LANES))
    for block in range(list_ref.shape[1] // LANES):
        hits = jnp.where(ends[0:1, :] == slot_of + block * LANES, 1.0, 0.0) + jnp.where(
            ends[1:2, :] == slot_of + block * LANES, 1.0, 0.0
        )
        tally = jnp.sum(hits, axis=1, keepdims=True).reshape(owners, per_owner, 1)
        named = list_ref[0:1, block * LANES : (block + 1) * LANES].astype(F32)
        named = jnp.sum(jnp.where(diagonal, named, 0.0), axis=1, keepdims=True)
        named = named.reshape(owners, per_owner, 1)
        first = dot(hits.astype(BF16), head, NT).reshape(owners, per_owner, LANES)
        split = hits.reshape(owners, per_owner, LANES)
        both = jnp.concatenate(
            [
                split[:, :low].reshape(owners * low, LANES),
                split[:, low:].reshape(owners * low, LANES),
            ],
            axis=1,
        ).astype(BF16)
        second = dot(both, tails, NT).reshape(owners, low, LANES)
        second = jnp.where(lane == rest, tally[:, :low], second)
        second = jnp.where(lane == rest + 1, named[:, :low], second)
        second = jnp.where(lane == HALF + rest, tally[:, low:], second)
        second = jnp.where(lane == HALF + rest + 1, named[:, low:], second)
        spot = slice(block * owners, (block + 1) * owners)
        out_ref[spot, 0:per_owner, :] = first.astype(BF16)
        out_ref[spot, per_owner:, :] = second.astype(BF16)


def pick(tails, column, nodes):
    column = tails[:, column : column + 1].astype(F32).astype(jnp.int32)
    return jnp.where(column == lane_index((tails.shape[0], nodes)), 1.0, 0.0).astype(BF16)


CHUNK = 16


def mean_body(rest, nodes, got_ref, out_ref):
    low = got_ref.shape[1] // 3
    size = CHUNK * low
    sum_low = jnp.zeros((nodes, 2 * LANES), F32)
    sum_high = jnp.zeros((nodes, 2 * LANES), F32)
    for start in range(0, got_ref.shape[0], CHUNK):
        spot = slice(start, start + CHUNK)
        tails = got_ref[spot, 2 * low :, :].reshape(size, LANES)
        heads = got_ref[spot, 0:low, :].reshape(size, LANES)
        pick_low = pick(tails, rest + 1, nodes)
        sum_low += dot(pick_low, jnp.concatenate([heads, tails], axis=1), TN)
        heads = got_ref[spot, low : 2 * low, :].reshape(size, LANES)
        pick_high = pick(tails, HALF + rest + 1, nodes)
        sum_high += dot(pick_high, jnp.concatenate([heads, tails], axis=1), TN)
    head = sum_low[:, :LANES] + sum_high[:, :LANES]
    tail = sum_low[:, LANES:] + pltpu.roll(sum_high[:, LANES:], HALF, 1)
    count = jnp.maximum(tail[:, rest : rest + 1], 1.0)
    head = head / count
    tail = jnp.where(lane_index(tail.shape) <= rest, tail / count, 0.0)
    cut = nodes // 2
    tail = jnp.where(
        lane_index((cut, LANES)) < HALF, tail[:cut], pltpu.roll(tail[cut:], HALF, 1)
    )
    for part in range(out_ref.shape[0]):
        out_ref[part, 0:nodes, :] = head.astype(BF16)
        out_ref[part, nodes:, :] = tail.astype(BF16)


def rows_body(
    rest,
    section_ref,
    mean_ref,
    got_ref,
    memory_ref,
    head_w_ref,
    low_w_ref,
    high_w_ref,
    gate_ref,
    bias_ref,
    rows_ref,
    memory_out_ref,
):
    nodes, width = memory_ref.shape
    section = section_ref[0]
    cut = nodes // 2
    state = memory_ref[...]
    for batch in range(mean_ref.shape[0]):
        tail = mean_ref[batch, nodes:, :]
        message = dot(mean_ref[batch, 0:nodes, :], head_w_ref[...]) + jnp.concatenate(
            [dot(tail, low_w_ref[...]), dot(tail, high_w_ref[...])], axis=0
        )
        touched = jnp.concatenate(
            [
                tail[:, rest : rest + 1].astype(F32),
                tail[:, HALF + rest : HALF + rest + 1].astype(F32),
            ],
            axis=0,
        )
        gate = dot(message.astype(BF16), gate_ref[...]) + bias_ref[...]
        update = jax.nn.sigmoid(gate[:, :width]) * jnp.where(touched > 0.5, 1.0, 0.0)
        after = (1.0 - update) * state + update * jnp.tanh(gate[:, width:])

        @pl.when(section == batch)
        def _():
            memory_out_ref[...] = after

        state = jnp.where(section > batch, after, state)
    before = state.astype(BF16)
    low = got_ref.shape[1] // 3
    size = CHUNK * low
    for start in range(0, got_ref.shape[0], CHUNK):
        spot = slice(start, start + CHUNK)
        tails = got_ref[spot, 2 * low :, :].reshape(size, LANES)
        rows = dot(pick(tails, rest + 1, nodes), before).astype(BF16)
        rows_ref[spot, 0:low, :] = rows.reshape(CHUNK, low, width)
        rows = dot(pick(tails, HALF + rest + 1, nodes), before).astype(BF16)
        rows_ref[spot, low:, :] = rows.reshape(CHUNK, low, width)


def event_body(
    rows_ref,
    ends_ref,
    near_ref,
    cos_ref,
    cot_ref,
    attn_ref,
    pred_ref,
    pred_flip_ref,
    pred_out_ref,
    scores_ref,
    grads_ref,
    flip_ref,
    value_ref,
):
    slots, width = rows_ref.shape
    events = ends_ref.shape[1]
    near_count = near_ref.shape[0] // 2
    pair = 2 * events
    head_dim = width // HEADS
    for start in range(0, slots, width):
        flip_ref[:, start : start + width] = rows_ref[start : start + width, :].T
    slot_of = lax.broadcasted_iota(jnp.int32, (slots, pair), 0)

    def fetch(index):
        return dot(flip_ref[...], jnp.where(slot_of == index, 1.0, 0.0).astype(BF16))

    own = fetch(jnp.concatenate([ends_ref[0:1, :], ends_ref[1:2, :]], axis=1))
    query = dot(attn_ref[0], own.astype(BF16)) * (1.0 / math.sqrt(head_dim))
    logits = []
    for near in range(near_count):
        index = jnp.concatenate(
            [near_ref[near : near + 1, :], near_ref[near_count + near : near_count + near + 1, :]],
            axis=1,
        )
        feat = fetch(index) + cos_ref[:, near * pair : (near + 1) * pair]
        feat = feat.astype(BF16)
        match = query * dot(attn_ref[1], feat)
        logits.append(
            [
                jnp.sum(match[head * head_dim : (head + 1) * head_dim], axis=0, keepdims=True)
                for head in range(HEADS)
            ]
        )
        value_ref[near] = dot(attn_ref[2], feat)
    mixed = []
    for head in range(HEADS):
        top = logits[0][head]
        for near in range(1, near_count):
            top = jnp.maximum(top, logits[near][head])
        powers = [jnp.exp(logits[near][head] - top) for near in range(near_count)]
        total = powers[0]
        for near in range(1, near_count):
            total = total + powers[near]
        spot = slice(head * head_dim, (head + 1) * head_dim)
        part = (powers[0] / total) * value_ref[0, spot, :]
        for near in range(1, near_count):
            part = part + (powers[near] / total) * value_ref[near, spot, :]
        mixed.append(part)
    mixed = jnp.concatenate(mixed, axis=0).astype(BF16)
    state = (own + dot(attn_ref[3], mixed)).astype(BF16)
    source, target = state[:, :events], state[:, events:]
    pre = dot(pred_flip_ref[0], source) + dot(pred_flip_ref[1], target)
    gate = jax.nn.sigmoid(pre)
    pred_out = pred_out_ref[...]
    scores_ref[...] = jnp.sum(pre * gate * pred_out, axis=0, keepdims=True)
    slope = (cot_ref[...] * pred_out * (gate * (1.0 + pre * (1.0 - gate)))).astype(BF16)
    back = jnp.concatenate([dot(pred_ref[0], slope), dot(pred_ref[1], slope)], axis=1)
    grads_ref[0:width, :] = dot(mixed, back.astype(BF16), NT).astype(BF16)
    grads_ref[width : 2 * width, :] = dot(source, slope, NT).astype(BF16)
    grads_ref[2 * width :, :] = dot(target, slope, NT).astype(BF16)


def exchange(value, axis, groups=None):
    return lax.all_to_all(
        value, axis, split_axis=0, concat_axis=0, tiled=True, axis_index_groups=groups
    )


def sum_everywhere(grads, columns, rings):
    plane = [
        [section * columns * rings + ring * columns + column for section in range(lax.axis_size("tm")) for column in range(columns)]
        for ring in range(rings)
    ]
    line = [[ring * columns + column for ring in range(rings)] for column in range(columns)]
    peers = len(plane[0])
    rows, width = grads.shape
    own = rows // peers
    pieces = exchange(grads.reshape(peers, own, width), ("tm", "dp"), plane)
    mine = jnp.sum(pieces.astype(F32), axis=0).astype(BF16)
    pieces = exchange(jnp.broadcast_to(mine[None], (rings, own, width)), "dp", line)
    mine = jnp.sum(pieces.astype(F32), axis=0).astype(BF16)
    whole = exchange(jnp.broadcast_to(mine[None], (peers, own, width)), ("tm", "dp"), plane)
    return whole.reshape(rows, width).astype(F32)


def per_device(
    edge_feat,
    endpoint_slots,
    neighbor_slots,
    neighbor_gap,
    score_grad,
    node_list,
    memory0,
    msg_weight,
    gate_weight,
    gate_bias,
    omega,
    attn_weights,
    pred_weights,
    pred_out,
):
    groups = lax.axis_size("dp")
    batches = lax.axis_size("tm")
    nodes, width = memory0.shape
    list_len = node_list.shape[2]
    per_owner = list_len // groups
    features = edge_feat.shape[2]
    rest = features - LANES
    events = endpoint_slots.shape[2]
    near_count = neighbor_slots.shape[1] // 2
    sent = dense_call(
        pack_body,
        jax.ShapeDtypeStruct((groups, per_owner * 3 // 2, LANES), BF16),
        (jnp.swapaxes(edge_feat[0], 0, 1), endpoint_slots[0], node_list[0]),
        [pltpu.VMEM((HALF, LANES), F32)],
    )
    got = exchange(sent, "dp")
    gaps = neighbor_gap[0].reshape(2, near_count, events)
    gaps = jnp.swapaxes(gaps, 0, 1).reshape(1, 2 * near_count * events).astype(F32)
    cosines = lax.optimization_barrier(jnp.cos(omega[:, None] * gaps))
    means = dense_call(
        lambda *refs: mean_body(rest, nodes, *refs),
        jax.ShapeDtypeStruct((batches, nodes + nodes // 2, LANES), BF16),
        (got,),
    )
    means = exchange(means, "tm")
    tail_w = jnp.pad(msg_weight[LANES:], ((0, HALF - rest), (0, 0)))
    section = lax.axis_index("tm").astype(jnp.int32)
    rows, new_memory = pl.pallas_call(
        lambda *refs: rows_body(rest, *refs),
        out_shape=(
            jax.ShapeDtypeStruct((groups, per_owner, width), BF16),
            jax.ShapeDtypeStruct((nodes, width), F32),
        ),
        in_specs=[pl.BlockSpec(memory_space=pltpu.SMEM)]
        + [pl.BlockSpec(memory_space=pltpu.VMEM)] * 8,
        compiler_params=PARAMS,
    )(
        section[None],
        means,
        got,
        memory0,
        msg_weight[:LANES],
        jnp.pad(tail_w, ((0, HALF), (0, 0))),
        jnp.pad(tail_w, ((HALF, 0), (0, 0))),
        gate_weight,
        gate_bias[None],
    )
    slot_rows = exchange(rows, "dp").reshape(list_len, width)
    scores, grads = dense_call(
        event_body,
        (
            jax.ShapeDtypeStruct((1, events), F32),
            jax.ShapeDtypeStruct((3 * width, width), BF16),
        ),
        (
            slot_rows,
            endpoint_slots[0],
            neighbor_slots[0],
            cosines,
            score_grad,
            jnp.swapaxes(attn_weights, 1, 2),
            pred_weights,
            jnp.swapaxes(pred_weights, 1, 2),
            pred_out[:, None],
        ),
        [
            pltpu.VMEM((width, list_len), BF16),
            pltpu.VMEM((near_count, width, 2 * events), F32),
        ],
    )
    columns = 4
    grads = sum_everywhere(grads, columns, groups // columns)
    grads = grads.reshape(3, width, width)
    return (scores, new_memory[None], grads[0], grads[1:])


def solution(mesh):
    in_specs = (
        P("tm", "dp", None),
        P("tm", None, "dp"),
        P("tm", None, "dp"),
        P("tm", None, "dp"),
        P("tm", "dp"),
        P("tm", "dp", None),
        P("dp", None),
        P(),
        P(),
        P(),
        P(),
        P(),
        P(),
        P(),
    )
    out_specs = (P("tm", "dp"), P("tm", "dp", None), P(), P())
    return jax.shard_map(
        per_device, mesh=mesh, in_specs=in_specs, out_specs=out_specs, check_vma=False
    )
```

```python
import math

import jax
import jax.numpy as jnp
from jax import lax
from jax.experimental import pallas as pl
from jax.experimental.pallas import tpu as pltpu
from jax.sharding import PartitionSpec as P

HEADS = 2
LANES = 128
HALF = LANES // 2
NT = (((1,), (1,)), ((), ()))
TN = (((0,), (0,)), ((), ()))
F32 = jnp.float32
BF16 = jnp.bfloat16
PARAMS = pltpu.CompilerParams(vmem_limit_bytes=12 * 1024 * 1024)
ALONE = pltpu.CompilerParams(vmem_limit_bytes=63 * 1024 * 1024)


def lane_index(shape):
    return lax.broadcasted_iota(jnp.int32, shape, len(shape) - 1)


def dot(left, right, dims=(((1,), (0,)), ((), ()))):
    return lax.dot_general(left, right, dims, preferred_element_type=F32)


def dense_call(body, out_shape, args, scratch=()):
    return pl.pallas_call(
        body,
        out_shape=out_shape,
        in_specs=[pl.BlockSpec(memory_space=pltpu.VMEM)] * len(args),
        scratch_shapes=list(scratch),
        compiler_params=PARAMS,
    )(*args)


def copies(sources, targets, sems):
    return [
        pltpu.make_async_copy(source, target, sems.at[index])
        for index, (source, target) in enumerate(zip(sources, targets))
    ]


def load(sources, targets, sems):
    started = copies(sources, targets, sems)
    for copy in started:
        copy.start()
    for copy in started:
        copy.wait()


def pack_body(feat_hbm, ends_hbm, list_hbm, out_ref, wide_ref, feat_ref, ends_ref, list_ref, sems):
    load((feat_hbm, ends_hbm, list_hbm), (feat_ref, ends_ref, list_ref), sems)
    rest = feat_ref.shape[0] - LANES
    wide_ref[...] = jnp.zeros_like(wide_ref)
    wide_ref[0:rest, :] = feat_ref[LANES:, :].astype(F32)
    tail = wide_ref[...].astype(BF16)
    empty = jnp.zeros_like(tail)
    tails = jnp.concatenate(
        [
            jnp.concatenate([tail, empty], axis=0),
            jnp.concatenate([empty, tail], axis=0),
        ],
        axis=1,
    )
    head = feat_ref[0:LANES, :]
    per_owner = out_ref.shape[1] * 2 // 3
    low = per_owner // 2
    owners = LANES // per_owner
    slot_of = lax.broadcasted_iota(jnp.int32, (LANES, LANES), 0)
    diagonal = slot_of == lane_index((LANES, LANES))
    ends = ends_ref[...]
    lane = lane_index((1, 1, LANES))
    for block in range(list_ref.shape[1] // LANES):
        hits = jnp.where(ends[0:1, :] == slot_of + block * LANES, 1.0, 0.0) + jnp.where(
            ends[1:2, :] == slot_of + block * LANES, 1.0, 0.0
        )
        tally = jnp.sum(hits, axis=1, keepdims=True).reshape(owners, per_owner, 1)
        named = list_ref[0:1, block * LANES : (block + 1) * LANES].astype(F32)
        named = jnp.sum(jnp.where(diagonal, named, 0.0), axis=1, keepdims=True)
        named = named.reshape(owners, per_owner, 1)
        first = dot(hits.astype(BF16), head, NT).reshape(owners, per_owner, LANES)
        split = hits.reshape(owners, per_owner, LANES)
        both = jnp.concatenate(
            [
                split[:, :low].reshape(owners * low, LANES),
                split[:, low:].reshape(owners * low, LANES),
            ],
            axis=1,
        ).astype(BF16)
        second = dot(both, tails, NT).reshape(owners, low, LANES)
        second = jnp.where(lane == rest, tally[:, :low], second)
        second = jnp.where(lane == rest + 1, named[:, :low], second)
        second = jnp.where(lane == HALF + rest, tally[:, low:], second)
        second = jnp.where(lane == HALF + rest + 1, named[:, low:], second)
        spot = slice(block * owners, (block + 1) * owners)
        out_ref[spot, 0:per_owner, :] = first.astype(BF16)
        out_ref[spot, per_owner:, :] = second.astype(BF16)


def pick(tails, column, nodes):
    column = tails[:, column : column + 1].astype(F32).astype(jnp.int32)
    return jnp.where(column == lane_index((tails.shape[0], nodes)), 1.0, 0.0).astype(BF16)


CHUNK = 16


def mean_body(rest, nodes, got_ref, out_ref):
    low = got_ref.shape[1] // 3
    size = CHUNK * low
    sum_low = jnp.zeros((nodes, 2 * LANES), F32)
    sum_high = jnp.zeros((nodes, 2 * LANES), F32)
    for start in range(0, got_ref.shape[0], CHUNK):
        spot = slice(start, start + CHUNK)
        tails = got_ref[spot, 2 * low :, :].reshape(size, LANES)
        heads = got_ref[spot, 0:low, :].reshape(size, LANES)
        pick_low = pick(tails, rest + 1, nodes)
        sum_low += dot(pick_low, jnp.concatenate([heads, tails], axis=1), TN)
        heads = got_ref[spot, low : 2 * low, :].reshape(size, LANES)
        pick_high = pick(tails, HALF + rest + 1, nodes)
        sum_high += dot(pick_high, jnp.concatenate([heads, tails], axis=1), TN)
    head = sum_low[:, :LANES] + sum_high[:, :LANES]
    tail = sum_low[:, LANES:] + pltpu.roll(sum_high[:, LANES:], HALF, 1)
    count = jnp.maximum(tail[:, rest : rest + 1], 1.0)
    head = head / count
    tail = jnp.where(lane_index(tail.shape) <= rest, tail / count, 0.0)
    cut = nodes // 2
    tail = jnp.where(
        lane_index((cut, LANES)) < HALF, tail[:cut], pltpu.roll(tail[cut:], HALF, 1)
    )
    for part in range(out_ref.shape[0]):
        out_ref[part, 0:nodes, :] = head.astype(BF16)
        out_ref[part, nodes:, :] = tail.astype(BF16)


def gates(rest, head, tail, head_w_ref, low_w_ref, high_w_ref, gate_ref, bias_ref):
    width = head_w_ref.shape[1]
    message = dot(head, head_w_ref[...]) + jnp.concatenate(
        [dot(tail, low_w_ref[...]), dot(tail, high_w_ref[...])], axis=0
    )
    touched = jnp.concatenate(
        [
            tail[:, rest : rest + 1].astype(F32),
            tail[:, HALF + rest : HALF + rest + 1].astype(F32),
        ],
        axis=0,
    )
    gate = dot(message.astype(BF16), gate_ref[...]) + bias_ref[...]
    update = jax.nn.sigmoid(gate[:, :width]) * jnp.where(touched > 0.5, 1.0, 0.0)
    return 1.0 - update, update * jnp.tanh(gate[:, width:])


def advance(rest, section, mean_ref, batches, memory_ref, weights):
    nodes = memory_ref.shape[0]
    state = memory_ref[...]
    for batch in range(batches):
        head, tail = mean_ref[batch, 0:nodes, :], mean_ref[batch, nodes:, :]
        decay, inject = gates(rest, head, tail, *weights)
        state = jnp.where(section > batch, decay * state + inject, state)
    return state


def rows_body(rest, section_ref, mean_ref, got_ref, memory_ref, *refs):
    weights, rows_ref = refs[:-1], refs[-1]
    nodes, width = memory_ref.shape
    batches = mean_ref.shape[0] - 1
    before = advance(rest, section_ref[0], mean_ref, batches, memory_ref, weights).astype(BF16)
    low = got_ref.shape[1] // 3
    size = CHUNK * low
    for start in range(0, got_ref.shape[0], CHUNK):
        spot = slice(start, start + CHUNK)
        tails = got_ref[spot, 2 * low :, :].reshape(size, LANES)
        rows = dot(pick(tails, rest + 1, nodes), before).astype(BF16)
        rows_ref[spot, 0:low, :] = rows.reshape(CHUNK, low, width)
        rows = dot(pick(tails, HALF + rest + 1, nodes), before).astype(BF16)
        rows_ref[spot, low:, :] = rows.reshape(CHUNK, low, width)


def memory_body(rest, section_ref, mean_ref, memory_ref, *refs):
    weights, out_ref = refs[:-1], refs[-1]
    out_ref[...] = advance(rest, section_ref[0] + 1, mean_ref, mean_ref.shape[0], memory_ref, weights)


def event_body(*refs):
    sources, (scores_ref, grads_ref), targets = refs[:8], refs[8:10], refs[10:18]
    feat_ref, sems = refs[18:]
    rows_ref, ends_ref, near_ref, cos_ref, cot_ref, attn_ref, pred_ref, pred_out_ref = targets
    started = copies(sources, targets, sems)
    rows_copy, ends_copy, near_copy, cos_copy, cot_copy, attn_copy, pred_copy, out_copy = started
    for copy in (ends_copy, rows_copy, near_copy, cos_copy, attn_copy, cot_copy, out_copy, pred_copy):
        copy.start()
    ends_copy.wait()
    rows_copy.wait()
    slots, width = rows_ref.shape
    events = ends_ref.shape[1]
    pair = 2 * events
    near_count = near_ref.shape[0] // 2
    head_dim = width // HEADS
    diagonal = lax.broadcasted_iota(jnp.int32, (events, events), 0) == lane_index((events, events))

    def upright(index):
        index = jnp.where(diagonal, index.astype(F32), 0.0)
        return jnp.sum(index, axis=1, keepdims=True).astype(jnp.int32)

    def fetch(source, target):
        index = jnp.concatenate([upright(source), upright(target)], axis=0)
        lanes = lane_index((pair, slots))
        return dot(jnp.where(index == lanes, 1.0, 0.0).astype(BF16), rows_ref[...])

    own = fetch(ends_ref[0:1, :], ends_ref[1:2, :])
    near_copy.wait()
    for near in range(near_count):
        spot = slice(near * pair, (near + 1) * pair)
        other = near_count + near
        feat = fetch(near_ref[near : near + 1, :], near_ref[other : other + 1, :])
        if near == 0:
            cos_copy.wait()
        feat_ref[spot, :] = (feat + cos_ref[spot, :]).astype(BF16)
    attn_copy.wait()
    query = dot(own.astype(BF16), attn_ref[0]) * (1.0 / math.sqrt(head_dim))
    keys = dot(feat_ref[...], attn_ref[1])
    logits = [[] for _ in range(HEADS)]
    for near in range(near_count):
        match = query * keys[near * pair : (near + 1) * pair]
        for head in range(HEADS):
            part = match[:, head * head_dim : (head + 1) * head_dim]
            logits[head].append(jnp.sum(part, axis=1, keepdims=True))
    values = dot(feat_ref[...], attn_ref[2])
    mixed = []
    for head in range(HEADS):
        top = logits[head][0]
        for near in range(1, near_count):
            top = jnp.maximum(top, logits[head][near])
        powers = [jnp.exp(logit - top) for logit in logits[head]]
        total = powers[0]
        for near in range(1, near_count):
            total = total + powers[near]
        part = jnp.zeros((pair, head_dim), F32)
        for near in range(near_count):
            value = values[near * pair : (near + 1) * pair, head * head_dim : (head + 1) * head_dim]
            part = part + (powers[near] / total) * value
        mixed.append(part)
    mixed = jnp.concatenate(mixed, axis=1).astype(BF16)
    state = (own + dot(mixed, attn_ref[3])).astype(BF16)
    source, target = state[:events], state[events:]
    cot_copy.wait()
    out_copy.wait()
    pred_copy.wait()
    pre = dot(source, pred_ref[0]) + dot(target, pred_ref[1])
    gate = jax.nn.sigmoid(pre)
    pred_out = pred_out_ref[...]
    column = jnp.sum(pre * gate * pred_out, axis=1, keepdims=True)
    scores_ref[...] = jnp.sum(jnp.where(diagonal, column, 0.0), axis=0, keepdims=True)
    cot = jnp.sum(jnp.where(diagonal, cot_ref[...], 0.0), axis=1, keepdims=True)
    slope = (cot * pred_out * (gate * (1.0 + pre * (1.0 - gate)))).astype(BF16)
    back = jnp.concatenate([dot(slope, pred_ref[0], NT), dot(slope, pred_ref[1], NT)], axis=0)
    grads_ref[0:width, :] = dot(mixed, back.astype(BF16), TN).astype(BF16)
    grads_ref[width : 2 * width, :] = dot(source, slope, TN).astype(BF16)
    grads_ref[2 * width :, :] = dot(target, slope, TN).astype(BF16)


def grads_body(whole_ref, first_ref, rest_ref):
    width = first_ref.shape[0]
    whole = whole_ref[...].astype(F32).reshape(3 * width, width)
    first_ref[...] = whole[:width]
    for part in range(2):
        rest_ref[part] = whole[(part + 1) * width : (part + 2) * width]


def exchange(value, axis, groups=None):
    return lax.all_to_all(
        value, axis, split_axis=0, concat_axis=0, tiled=True, axis_index_groups=groups
    )


def sum_everywhere(grads, columns, rings):
    sections = lax.axis_size("tm")
    plane = [
        [
            (section * rings + ring) * columns + column
            for section in range(sections)
            for column in range(columns)
        ]
        for ring in range(rings)
    ]
    line = [[ring * columns + column for ring in range(rings)] for column in range(columns)]
    peers = len(plane[0])
    rows, width = grads.shape
    own = rows // peers
    pieces = exchange(grads.reshape(peers, own, width), ("tm", "dp"), plane)
    mine = jnp.sum(pieces.astype(F32), axis=0).astype(BF16)
    pieces = exchange(jnp.broadcast_to(mine[None], (rings, own, width)), "dp", line)
    mine = jnp.sum(pieces.astype(F32), axis=0).astype(BF16)
    whole = exchange(jnp.broadcast_to(mine[None], (peers, own, width)), ("tm", "dp"), plane)
    return dense_call(
        grads_body,
        (
            jax.ShapeDtypeStruct((width, width), F32),
            jax.ShapeDtypeStruct((rows // width - 1, width, width), F32),
        ),
        (whole,),
    )


def per_device(
    edge_feat,
    endpoint_slots,
    neighbor_slots,
    neighbor_gap,
    score_grad,
    node_list,
    memory0,
    msg_weight,
    gate_weight,
    gate_bias,
    omega,
    attn_weights,
    pred_weights,
    pred_out,
):
    groups = lax.axis_size("dp")
    batches = lax.axis_size("tm")
    nodes, width = memory0.shape
    list_len = node_list.shape[2]
    per_owner = list_len // groups
    features = edge_feat.shape[2]
    rest = features - LANES
    events = endpoint_slots.shape[2]
    near_count = neighbor_slots.shape[1] // 2
    sent = pl.pallas_call(
        pack_body,
        out_shape=jax.ShapeDtypeStruct((groups, per_owner * 3 // 2, LANES), BF16),
        in_specs=[pl.BlockSpec(memory_space=pltpu.HBM)] * 3,
        scratch_shapes=[
            pltpu.VMEM((HALF, LANES), F32),
            pltpu.VMEM((features, events), BF16),
            pltpu.VMEM((2, events), jnp.int32),
            pltpu.VMEM((1, list_len), jnp.int32),
            pltpu.SemaphoreType.DMA((3,)),
        ],
        compiler_params=ALONE,
    )(jnp.swapaxes(edge_feat[0], 0, 1), endpoint_slots[0], node_list[0])
    got = exchange(sent, "dp")
    pairs = 2 * near_count * events

    def by_neighbour(value):
        return jnp.swapaxes(value[0].reshape(2, near_count, events), 0, 1).reshape(pairs, 1)

    cosines = jnp.cos(by_neighbour(neighbor_gap).astype(F32) * omega[None, :])
    means = dense_call(
        lambda *refs: mean_body(rest, nodes, *refs),
        jax.ShapeDtypeStruct((batches, nodes + nodes // 2, LANES), BF16),
        (got,),
    )
    means = exchange(means, "tm")
    tail_w = jnp.pad(msg_weight[LANES:], ((0, HALF - rest), (0, 0)))
    section = lax.axis_index("tm").astype(jnp.int32)
    weights = (
        msg_weight[:LANES],
        jnp.pad(tail_w, ((0, HALF), (0, 0))),
        jnp.pad(tail_w, ((HALF, 0), (0, 0))),
        gate_weight,
        gate_bias[None],
    )

    def section_call(body, out_shape, args):
        return pl.pallas_call(
            lambda *refs: body(rest, *refs),
            out_shape=out_shape,
            in_specs=[pl.BlockSpec(memory_space=pltpu.SMEM)]
            + [pl.BlockSpec(memory_space=pltpu.VMEM)] * (len(args) + len(weights)),
            compiler_params=PARAMS,
        )(section[None], *args, *weights)

    rows = section_call(
        rows_body,
        jax.ShapeDtypeStruct((groups, per_owner, width), BF16),
        (means, got, memory0),
    )
    new_memory = section_call(
        memory_body, jax.ShapeDtypeStruct((nodes, width), F32), (means, memory0)
    )
    slot_rows = exchange(rows, "dp").reshape(list_len, width)
    cosines, new_memory = lax.optimization_barrier((cosines, new_memory))
    inputs = (
        slot_rows,
        endpoint_slots[0],
        neighbor_slots[0],
        cosines,
        score_grad,
        attn_weights,
        pred_weights,
        pred_out[None],
    )
    scores, grads = pl.pallas_call(
        event_body,
        out_shape=(
            jax.ShapeDtypeStruct((1, events), F32),
            jax.ShapeDtypeStruct((3 * width, width), BF16),
        ),
        in_specs=[pl.BlockSpec(memory_space=pltpu.HBM)] * len(inputs),
        scratch_shapes=[pltpu.VMEM(value.shape, value.dtype) for value in inputs]
        + [pltpu.VMEM((pairs, width), BF16), pltpu.SemaphoreType.DMA((len(inputs),))],
        compiler_params=ALONE,
    )(*inputs)
    columns = 4
    grad_out, grad_pair = sum_everywhere(grads, columns, groups // columns)
    return (scores, new_memory[None], grad_out, grad_pair)


def solution(mesh):
    in_specs = (
        P("tm", "dp", None),
        P("tm", None, "dp"),
        P("tm", None, "dp"),
        P("tm", None, "dp"),
        P("tm", "dp"),
        P("tm", "dp", None),
        P("dp", None),
        P(),
        P(),
        P(),
        P(),
        P(),
        P(),
        P(),
    )
    out_specs = (P("tm", "dp"), P("tm", "dp", None), P(), P())
    return jax.shard_map(
        per_device, mesh=mesh, in_specs=in_specs, out_specs=out_specs, check_vma=False
    )
```

```python
import math

import jax
import jax.numpy as jnp
from jax import lax
from jax.experimental import pallas as pl
from jax.experimental.pallas import tpu as pltpu
from jax.sharding import PartitionSpec as P

HEADS = 2
LANES = 128
HALF = LANES // 2
NT = (((1,), (1,)), ((), ()))
TN = (((0,), (0,)), ((), ()))
F32 = jnp.float32
BF16 = jnp.bfloat16
PARAMS = pltpu.CompilerParams(vmem_limit_bytes=12 * 1024 * 1024)
ALONE = pltpu.CompilerParams(vmem_limit_bytes=63 * 1024 * 1024)


def lane_index(shape):
    return lax.broadcasted_iota(jnp.int32, shape, len(shape) - 1)


def dot(left, right, dims=(((1,), (0,)), ((), ()))):
    return lax.dot_general(left, right, dims, preferred_element_type=F32)


def dense_call(body, out_shape, args, scratch=()):
    return pl.pallas_call(
        body,
        out_shape=out_shape,
        in_specs=[pl.BlockSpec(memory_space=pltpu.VMEM)] * len(args),
        scratch_shapes=list(scratch),
        compiler_params=PARAMS,
    )(*args)


def copies(sources, targets, sems):
    return [
        pltpu.make_async_copy(source, target, sems.at[index])
        for index, (source, target) in enumerate(zip(sources, targets))
    ]


def load(sources, targets, sems):
    started = copies(sources, targets, sems)
    for copy in started:
        copy.start()
    for copy in started:
        copy.wait()


WIRE = LANES + HALF
CHUNK = 16


def pack_body(per_owner, feat_hbm, ends_hbm, list_hbm, out_ref, *refs):
    wide_ref, rows_ref, feat_ref, ends_ref, list_ref, sems = refs
    load((feat_hbm, ends_hbm, list_hbm), (feat_ref, ends_ref, list_ref), sems)
    rest = feat_ref.shape[0] - LANES
    list_len = list_ref.shape[1]
    blocks = list_len // LANES
    slot_of = lax.broadcasted_iota(jnp.int32, (LANES, LANES), 0)
    diagonal = slot_of == lane_index((LANES, LANES))
    ends = ends_ref[...]
    found = [jnp.zeros((LANES, LANES), F32) for _ in range(2)]
    for block in range(blocks):
        named = list_ref[0:1, block * LANES : (block + 1) * LANES].astype(F32)
        rows_ref[block : block + 1, :] = named
        named = jnp.sum(jnp.where(diagonal, named, 0.0), axis=1, keepdims=True)
        for side in range(2):
            hit = ends[side : side + 1, :] == slot_of + block * LANES
            found[side] = found[side] + jnp.where(hit, named, 0.0)
    wide_ref[...] = jnp.zeros_like(wide_ref)
    wide_ref[0:rest, :] = feat_ref[LANES:, :].astype(F32)
    wide_ref[rest : rest + 1, :] = jnp.ones((1, LANES), F32)
    for side in range(2):
        spot = rest + 1 + 2 * side
        wide_ref[spot : spot + 1, :] = (ends[side : side + 1, :] // per_owner).astype(F32)
        wide_ref[spot + 1 : spot + 2, :] = jnp.sum(found[side], axis=0, keepdims=True)
    out_ref[0:LANES, :] = feat_ref[0:LANES, :]
    out_ref[LANES:WIRE, :] = wide_ref[...].astype(BF16)
    out_ref[WIRE:, :] = rows_ref[...].astype(BF16)


def sums_body(rest, nodes, ring_ref, got_ref, out_ref, rows_ref):
    rings = got_ref.shape[0]
    columns = out_ref.shape[0]
    ring = ring_ref[0]
    base = ring * columns * nodes
    node_of = lax.broadcasted_iota(jnp.int32, (columns * nodes, 2 * LANES), 0)
    total = jnp.zeros((columns * nodes, 2 * LANES), F32)

    def keys(part, side):
        spot = rest + 1 + 2 * side
        rows = got_ref[part, LANES:WIRE, :].astype(F32)
        key = rows[spot : spot + 1, :] * nodes + rows[spot + 1 : spot + 2, :]
        return key.astype(jnp.int32) - base

    for part in range(0, rings, 2):
        hits = jnp.zeros((columns * nodes, 2 * LANES), F32)
        for side in range(2):
            key = jnp.concatenate([keys(part, side), keys(part + 1, side)], axis=1)
            hits = hits + jnp.where(node_of == key, 1.0, 0.0)
        feats = []
        for source in (part, part + 1):
            tail = got_ref[source, LANES:WIRE, :]
            feats.append(jnp.concatenate([got_ref[source, 0:LANES, :], tail, tail], axis=0))
        total = total + dot(hits.astype(BF16), jnp.concatenate(feats, axis=1), NT)
    list_rows = lax.broadcasted_iota(jnp.int32, (rings, LANES), 0)
    for part in range(rings):
        named = jnp.where(list_rows == ring, got_ref[part, WIRE:, :].astype(F32), 0.0)
        rows_ref[part : part + 1, :] = jnp.sum(named, axis=0, keepdims=True)
    cut = nodes // 2
    lane = lane_index((cut, LANES))
    low_lane = lane < HALF
    spot = jnp.where(low_lane, lane, lane - HALF)
    for column in range(columns):
        mine = total[column * nodes : (column + 1) * nodes]
        tail = jnp.where(low_lane, mine[:cut, LANES:], mine[cut:, LANES:])
        high = jnp.floor(tail * (1.0 / LANES))
        tail = jnp.where(spot == rest, tail - high * LANES, tail)
        tail = jnp.where(spot == rest + 1, pltpu.roll(high, 1, 1), tail)
        out_ref[column, 0:LANES, :] = mine[:, :LANES].astype(BF16)
        out_ref[column, LANES:WIRE, :] = tail.astype(BF16)
        out_ref[column, WIRE:, :] = rows_ref[...].astype(BF16)


def mean_body(rest, nodes, got_ref, out_ref):
    total = got_ref[0, 0:WIRE, :].astype(F32)
    for column in range(1, got_ref.shape[0]):
        total = total + got_ref[column, 0:WIRE, :].astype(F32)
    cut = nodes // 2
    head, tail = total[:nodes], total[nodes:]

    def count(start):
        spot = start + rest
        return tail[:, spot : spot + 1] + LANES * tail[:, spot + 1 : spot + 2]

    low, high = count(0), count(HALF)
    low_safe, high_safe = jnp.maximum(low, 1.0), jnp.maximum(high, 1.0)
    head = jnp.concatenate([head[:cut] / low_safe, head[cut:] / high_safe], axis=0)
    lane = lane_index((cut, LANES))
    low_lane = lane < HALF
    spot = jnp.where(low_lane, lane, lane - HALF)
    touched = jnp.where(jnp.where(low_lane, low, high) > 0.5, 1.0, 0.0)
    tail = tail / jnp.where(low_lane, low_safe, high_safe)
    tail = jnp.where(spot < rest, tail, jnp.where(spot == rest, touched, 0.0))
    for part in range(out_ref.shape[0]):
        out_ref[part, 0:nodes, :] = head.astype(BF16)
        out_ref[part, nodes:, :] = tail.astype(BF16)


def pick_body(column_ref, got_ref, out_ref):
    columns = got_ref.shape[0]
    rings = got_ref.shape[1] - WIRE
    per_owner, nodes = out_ref.shape[1:]
    shift = lax.rem((columns - column_ref[0]) * per_owner, LANES)
    upright = lax.broadcasted_iota(jnp.int32, (per_owner, LANES), 0) == lane_index((per_owner, LANES))
    node_of = lane_index((per_owner, nodes))
    for column in range(columns):
        named = pltpu.roll(got_ref[column, WIRE:, :].astype(F32), shift, 1)
        for ring in range(rings):
            asked = jnp.where(upright, named[ring : ring + 1, :], 0.0)
            asked = jnp.sum(asked, axis=1, keepdims=True).astype(jnp.int32)
            hits = jnp.where(asked == node_of, 1.0, 0.0).astype(BF16)
            out_ref[ring * columns + column] = hits


def gates(rest, head, tail, head_w_ref, low_w_ref, high_w_ref, gate_ref, bias_ref):
    width = head_w_ref.shape[1]
    message = dot(head, head_w_ref[...]) + jnp.concatenate(
        [dot(tail, low_w_ref[...]), dot(tail, high_w_ref[...])], axis=0
    )
    touched = jnp.concatenate(
        [
            tail[:, rest : rest + 1].astype(F32),
            tail[:, HALF + rest : HALF + rest + 1].astype(F32),
        ],
        axis=0,
    )
    gate = dot(message.astype(BF16), gate_ref[...]) + bias_ref[...]
    update = jax.nn.sigmoid(gate[:, :width]) * jnp.where(touched > 0.5, 1.0, 0.0)
    return 1.0 - update, update * jnp.tanh(gate[:, width:])


def advance(rest, section, mean_ref, batches, memory_ref, weights):
    nodes = memory_ref.shape[0]
    state = memory_ref[...]
    for batch in range(batches):
        head, tail = mean_ref[batch, 0:nodes, :], mean_ref[batch, nodes:, :]
        decay, inject = gates(rest, head, tail, *weights)
        state = jnp.where(section > batch, decay * state + inject, state)
    return state


def rows_body(rest, section_ref, mean_ref, pick_ref, memory_ref, *refs):
    weights, rows_ref = refs[:-1], refs[-1]
    batches = mean_ref.shape[0] - 1
    before = advance(rest, section_ref[0], mean_ref, batches, memory_ref, weights).astype(BF16)
    groups, per_owner, nodes = pick_ref.shape
    for start in range(0, groups, CHUNK):
        spot = slice(start, start + CHUNK)
        picks = pick_ref[spot].reshape(CHUNK * per_owner, nodes)
        rows = dot(picks, before).astype(BF16)
        rows_ref[spot] = rows.reshape(CHUNK, per_owner, before.shape[1])


def memory_body(rest, section_ref, mean_ref, memory_ref, *refs):
    weights, out_ref = refs[:-1], refs[-1]
    out_ref[...] = advance(rest, section_ref[0] + 1, mean_ref, mean_ref.shape[0], memory_ref, weights)


def event_body(*refs):
    sources, (scores_ref, grads_ref), targets = refs[:8], refs[8:10], refs[10:18]
    feat_ref, sems = refs[18:]
    rows_ref, ends_ref, near_ref, cos_ref, cot_ref, attn_ref, pred_ref, pred_out_ref = targets
    started = copies(sources, targets, sems)
    rows_copy, ends_copy, near_copy, cos_copy, cot_copy, attn_copy, pred_copy, out_copy = started
    for copy in (ends_copy, rows_copy, near_copy, cos_copy, attn_copy, cot_copy, out_copy, pred_copy):
        copy.start()
    ends_copy.wait()
    rows_copy.wait()
    slots, width = rows_ref.shape
    events = ends_ref.shape[1]
    pair = 2 * events
    near_count = near_ref.shape[0] // 2
    head_dim = width // HEADS
    diagonal = lax.broadcasted_iota(jnp.int32, (events, events), 0) == lane_index((events, events))

    def upright(index):
        index = jnp.where(diagonal, index.astype(F32), 0.0)
        return jnp.sum(index, axis=1, keepdims=True).astype(jnp.int32)

    def fetch(source, target):
        index = jnp.concatenate([upright(source), upright(target)], axis=0)
        lanes = lane_index((pair, slots))
        return dot(jnp.where(index == lanes, 1.0, 0.0).astype(BF16), rows_ref[...])

    own = fetch(ends_ref[0:1, :], ends_ref[1:2, :])
    near_copy.wait()
    for near in range(near_count):
        spot = slice(near * pair, (near + 1) * pair)
        other = near_count + near
        feat = fetch(near_ref[near : near + 1, :], near_ref[other : other + 1, :])
        if near == 0:
            cos_copy.wait()
        feat_ref[spot, :] = (feat + cos_ref[spot, :]).astype(BF16)
    attn_copy.wait()
    query = dot(own.astype(BF16), attn_ref[0]) * (1.0 / math.sqrt(head_dim))
    keys = dot(feat_ref[...], attn_ref[1])
    logits = [[] for _ in range(HEADS)]
    for near in range(near_count):
        match = query * keys[near * pair : (near + 1) * pair]
        for head in range(HEADS):
            part = match[:, head * head_dim : (head + 1) * head_dim]
            logits[head].append(jnp.sum(part, axis=1, keepdims=True))
    values = dot(feat_ref[...], attn_ref[2])
    mixed = []
    for head in range(HEADS):
        top = logits[head][0]
        for near in range(1, near_count):
            top = jnp.maximum(top, logits[head][near])
        powers = [jnp.exp(logit - top) for logit in logits[head]]
        total = powers[0]
        for near in range(1, near_count):
            total = total + powers[near]
        part = jnp.zeros((pair, head_dim), F32)
        for near in range(near_count):
            value = values[near * pair : (near + 1) * pair, head * head_dim : (head + 1) * head_dim]
            part = part + (powers[near] / total) * value
        mixed.append(part)
    mixed = jnp.concatenate(mixed, axis=1).astype(BF16)
    state = (own + dot(mixed, attn_ref[3])).astype(BF16)
    source, target = state[:events], state[events:]
    cot_copy.wait()
    out_copy.wait()
    pred_copy.wait()
    pre = dot(source, pred_ref[0]) + dot(target, pred_ref[1])
    gate = jax.nn.sigmoid(pre)
    pred_out = pred_out_ref[...]
    column = jnp.sum(pre * gate * pred_out, axis=1, keepdims=True)
    scores_ref[...] = jnp.sum(jnp.where(diagonal, column, 0.0), axis=0, keepdims=True)
    cot = jnp.sum(jnp.where(diagonal, cot_ref[...], 0.0), axis=1, keepdims=True)
    slope = (cot * pred_out * (gate * (1.0 + pre * (1.0 - gate)))).astype(BF16)
    back = jnp.concatenate([dot(slope, pred_ref[0], NT), dot(slope, pred_ref[1], NT)], axis=0)
    grads_ref[0:width, :] = dot(mixed, back.astype(BF16), TN).astype(BF16)
    grads_ref[width : 2 * width, :] = dot(source, slope, TN).astype(BF16)
    grads_ref[2 * width :, :] = dot(target, slope, TN).astype(BF16)


def grads_body(whole_ref, first_ref, rest_ref):
    width = first_ref.shape[0]
    whole = whole_ref[...].astype(F32).reshape(3 * width, width)
    first_ref[...] = whole[:width]
    for part in range(2):
        rest_ref[part] = whole[(part + 1) * width : (part + 2) * width]


def exchange(value, axis, groups=None):
    return lax.all_to_all(
        value, axis, split_axis=0, concat_axis=0, tiled=True, axis_index_groups=groups
    )


def sum_everywhere(grads, columns, rings):
    sections = lax.axis_size("tm")
    plane = [
        [
            (section * rings + ring) * columns + column
            for section in range(sections)
            for column in range(columns)
        ]
        for ring in range(rings)
    ]
    line = [[ring * columns + column for ring in range(rings)] for column in range(columns)]
    peers = len(plane[0])
    rows, width = grads.shape
    own = rows // peers
    pieces = exchange(grads.reshape(peers, own, width), ("tm", "dp"), plane)
    mine = jnp.sum(pieces.astype(F32), axis=0).astype(BF16)
    pieces = exchange(jnp.broadcast_to(mine[None], (rings, own, width)), "dp", line)
    mine = jnp.sum(pieces.astype(F32), axis=0).astype(BF16)
    whole = exchange(jnp.broadcast_to(mine[None], (peers, own, width)), ("tm", "dp"), plane)
    return dense_call(
        grads_body,
        (
            jax.ShapeDtypeStruct((width, width), F32),
            jax.ShapeDtypeStruct((rows // width - 1, width, width), F32),
        ),
        (whole,),
    )


def per_device(
    edge_feat,
    endpoint_slots,
    neighbor_slots,
    neighbor_gap,
    score_grad,
    node_list,
    memory0,
    msg_weight,
    gate_weight,
    gate_bias,
    omega,
    attn_weights,
    pred_weights,
    pred_out,
):
    groups = lax.axis_size("dp")
    batches = lax.axis_size("tm")
    nodes, width = memory0.shape
    list_len = node_list.shape[2]
    per_owner = list_len // groups
    features = edge_feat.shape[2]
    rest = features - LANES
    events = endpoint_slots.shape[2]
    near_count = neighbor_slots.shape[1] // 2
    columns = 4
    rings = groups // columns
    line = [[ring * columns + column for ring in range(rings)] for column in range(columns)]
    across = [[ring * columns + column for column in range(columns)] for ring in range(rings)]
    place = lax.axis_index("dp").astype(jnp.int32)
    blocks = list_len // LANES
    sent = pl.pallas_call(
        lambda *refs: pack_body(per_owner, *refs),
        out_shape=jax.ShapeDtypeStruct((WIRE + blocks, LANES), BF16),
        in_specs=[pl.BlockSpec(memory_space=pltpu.HBM)] * 3,
        scratch_shapes=[
            pltpu.VMEM((HALF, LANES), F32),
            pltpu.VMEM((blocks, LANES), F32),
            pltpu.VMEM((features, events), BF16),
            pltpu.VMEM((2, events), jnp.int32),
            pltpu.VMEM((1, list_len), jnp.int32),
            pltpu.SemaphoreType.DMA((3,)),
        ],
        compiler_params=ALONE,
    )(jnp.swapaxes(edge_feat[0], 0, 1), endpoint_slots[0], node_list[0])
    got = lax.all_gather(sent, "dp", axis=0, tiled=True, axis_index_groups=line)
    in_smem, in_vmem = pl.BlockSpec(memory_space=pltpu.SMEM), pl.BlockSpec(memory_space=pltpu.VMEM)
    sums = pl.pallas_call(
        lambda *refs: sums_body(rest, nodes, *refs),
        out_shape=jax.ShapeDtypeStruct((columns, WIRE + blocks, LANES), BF16),
        in_specs=[in_smem, in_vmem],
        scratch_shapes=[pltpu.VMEM((rings, LANES), F32)],
        compiler_params=PARAMS,
    )((place // columns)[None], got.reshape(rings, WIRE + blocks, LANES))
    got = exchange(sums, "dp", across)
    picks = pl.pallas_call(
        pick_body,
        out_shape=jax.ShapeDtypeStruct((groups, per_owner, nodes), BF16),
        in_specs=[in_smem, in_vmem],
        compiler_params=PARAMS,
    )((place % columns)[None], got)
    pairs = 2 * near_count * events

    def by_neighbour(value):
        return jnp.swapaxes(value[0].reshape(2, near_count, events), 0, 1).reshape(pairs, 1)

    cosines = jnp.cos(by_neighbour(neighbor_gap).astype(F32) * omega[None, :])
    means = dense_call(
        lambda *refs: mean_body(rest, nodes, *refs),
        jax.ShapeDtypeStruct((batches, nodes + nodes // 2, LANES), BF16),
        (got,),
    )
    means = exchange(means, "tm")
    tail_w = jnp.pad(msg_weight[LANES:], ((0, HALF - rest), (0, 0)))
    section = lax.axis_index("tm").astype(jnp.int32)
    weights = (
        msg_weight[:LANES],
        jnp.pad(tail_w, ((0, HALF), (0, 0))),
        jnp.pad(tail_w, ((HALF, 0), (0, 0))),
        gate_weight,
        gate_bias[None],
    )

    def section_call(body, out_shape, args):
        return pl.pallas_call(
            lambda *refs: body(rest, *refs),
            out_shape=out_shape,
            in_specs=[pl.BlockSpec(memory_space=pltpu.SMEM)]
            + [pl.BlockSpec(memory_space=pltpu.VMEM)] * (len(args) + len(weights)),
            compiler_params=PARAMS,
        )(section[None], *args, *weights)

    rows = section_call(
        rows_body,
        jax.ShapeDtypeStruct((groups, per_owner, width), BF16),
        (means, picks, memory0),
    )
    new_memory = section_call(
        memory_body, jax.ShapeDtypeStruct((nodes, width), F32), (means, memory0)
    )
    slot_rows = exchange(rows, "dp").reshape(list_len, width)
    cosines, new_memory = lax.optimization_barrier((cosines, new_memory))
    inputs = (
        slot_rows,
        endpoint_slots[0],
        neighbor_slots[0],
        cosines,
        score_grad,
        attn_weights,
        pred_weights,
        pred_out[None],
    )
    scores, grads = pl.pallas_call(
        event_body,
        out_shape=(
            jax.ShapeDtypeStruct((1, events), F32),
            jax.ShapeDtypeStruct((3 * width, width), BF16),
        ),
        in_specs=[pl.BlockSpec(memory_space=pltpu.HBM)] * len(inputs),
        scratch_shapes=[pltpu.VMEM(value.shape, value.dtype) for value in inputs]
        + [pltpu.VMEM((pairs, width), BF16), pltpu.SemaphoreType.DMA((len(inputs),))],
        compiler_params=ALONE,
    )(*inputs)
    grad_out, grad_pair = sum_everywhere(grads, columns, rings)
    return (scores, new_memory[None], grad_out, grad_pair)


def solution(mesh):
    in_specs = (
        P("tm", "dp", None),
        P("tm", None, "dp"),
        P("tm", None, "dp"),
        P("tm", None, "dp"),
        P("tm", "dp"),
        P("tm", "dp", None),
        P("dp", None),
        P(),
        P(),
        P(),
        P(),
        P(),
        P(),
        P(),
    )
    out_specs = (P("tm", "dp"), P("tm", "dp", None), P(), P())
    return jax.shard_map(
        per_device, mesh=mesh, in_specs=in_specs, out_specs=out_specs, check_vma=False
    )
```

```python
import math

import jax
import jax.numpy as jnp
from jax import lax
from jax.experimental import pallas as pl
from jax.experimental.pallas import tpu as pltpu
from jax.sharding import PartitionSpec as P

HEADS = 2
LANES = 128
HALF = LANES // 2
NT = (((1,), (1,)), ((), ()))
TN = (((0,), (0,)), ((), ()))
F32 = jnp.float32
BF16 = jnp.bfloat16
PARAMS = pltpu.CompilerParams(vmem_limit_bytes=12 * 1024 * 1024)
ALONE = pltpu.CompilerParams(vmem_limit_bytes=63 * 1024 * 1024)


def lane_index(shape):
    return lax.broadcasted_iota(jnp.int32, shape, len(shape) - 1)


def dot(left, right, dims=(((1,), (0,)), ((), ()))):
    return lax.dot_general(left, right, dims, preferred_element_type=F32)


def dense_call(body, out_shape, args, scratch=()):
    return pl.pallas_call(
        body,
        out_shape=out_shape,
        in_specs=[pl.BlockSpec(memory_space=pltpu.VMEM)] * len(args),
        scratch_shapes=list(scratch),
        compiler_params=PARAMS,
    )(*args)


def copies(sources, targets, sems):
    return [
        pltpu.make_async_copy(source, target, sems.at[index])
        for index, (source, target) in enumerate(zip(sources, targets))
    ]


def load(sources, targets, sems):
    started = copies(sources, targets, sems)
    for copy in started:
        copy.start()
    for copy in started:
        copy.wait()


WIRE = LANES + HALF


def pack_body(per_owner, feat_hbm, ends_hbm, list_hbm, out_ref, rows_ref, *refs):
    wide_ref, feat_ref, ends_ref, list_ref, sems = refs
    load((feat_hbm, ends_hbm, list_hbm), (feat_ref, ends_ref, list_ref), sems)
    rest = feat_ref.shape[0] - LANES
    hops = rows_ref.shape[0]
    slot_of = lax.broadcasted_iota(jnp.int32, (LANES, LANES), 0)
    diagonal = slot_of == lane_index((LANES, LANES))
    ends = ends_ref[...]
    found = [jnp.zeros((LANES, LANES), F32) for _ in range(2)]
    for block in range(list_ref.shape[1] // LANES):
        named = list_ref[0:1, block * LANES : (block + 1) * LANES].astype(F32)
        turn = block // hops
        rows_ref[block % hops, turn : turn + 1, :] = named
        named = jnp.sum(jnp.where(diagonal, named, 0.0), axis=1, keepdims=True)
        for side in range(2):
            hit = ends[side : side + 1, :] == slot_of + block * LANES
            found[side] = found[side] + jnp.where(hit, named, 0.0)
    wide_ref[...] = jnp.zeros_like(wide_ref)
    wide_ref[0:rest, :] = feat_ref[LANES:, :].astype(F32)
    wide_ref[rest : rest + 1, :] = jnp.ones((1, LANES), F32)
    for side in range(2):
        spot = rest + 1 + 2 * side
        wide_ref[spot : spot + 1, :] = (ends[side : side + 1, :] // per_owner).astype(F32)
        wide_ref[spot + 1 : spot + 2, :] = jnp.sum(found[side], axis=0, keepdims=True)
    out_ref[0:LANES, :] = feat_ref[0:LANES, :]
    out_ref[LANES:, :] = wide_ref[...].astype(BF16)


def sums_body(rest, nodes, turn_ref, got_ref, list_hbm, out_ref, list_ref, sem):
    copy = pltpu.make_async_copy(list_hbm, list_ref, sem)
    copy.start()
    turns = got_ref.shape[0]
    peers = out_ref.shape[0]
    hops = list_ref.shape[0]
    span = peers * nodes
    base = turn_ref[0] * span
    node_of = lax.broadcasted_iota(jnp.int32, (span, 2 * LANES), 0)
    total = jnp.zeros((span, 2 * LANES), F32)

    def keys(part, side):
        spot = rest + 1 + 2 * side
        rows = got_ref[part, LANES:, :].astype(F32)
        key = rows[spot : spot + 1, :] * nodes + rows[spot + 1 : spot + 2, :]
        return key.astype(jnp.int32) - base

    for part in range(0, turns, 2):
        hits = jnp.zeros((span, 2 * LANES), F32)
        for side in range(2):
            key = jnp.concatenate([keys(part, side), keys(part + 1, side)], axis=1)
            hits = hits + jnp.where(node_of == key, 1.0, 0.0)
        feats = []
        for source in (part, part + 1):
            tail = got_ref[source, LANES:, :]
            feats.append(jnp.concatenate([got_ref[source, 0:LANES, :], tail, tail], axis=0))
        total = total + dot(hits.astype(BF16), jnp.concatenate(feats, axis=1), NT)
    cut = nodes // 2
    lane = lane_index((cut, LANES))
    low_lane = lane < HALF
    spot = jnp.where(low_lane, lane, lane - HALF)
    copy.wait()
    for peer in range(peers):
        mine = total[peer * nodes : (peer + 1) * nodes]
        tail = jnp.where(low_lane, mine[:cut, LANES:], mine[cut:, LANES:])
        high = jnp.floor(tail * (1.0 / LANES))
        tail = jnp.where(spot == rest, tail - high * LANES, tail)
        tail = jnp.where(spot == rest + 1, pltpu.roll(high, 1, 1), tail)
        out_ref[peer, 0:LANES, :] = mine[:, :LANES].astype(BF16)
        out_ref[peer, LANES:WIRE, :] = tail.astype(BF16)
        named = list_ref[peer // (peers // hops)]
        out_ref[peer, WIRE:, :] = jnp.concatenate([named, named], axis=0).astype(BF16)


def mean_body(rest, nodes, got_ref, out_ref):
    total = got_ref[0, 0:WIRE, :].astype(F32)
    for column in range(1, got_ref.shape[0]):
        total = total + got_ref[column, 0:WIRE, :].astype(F32)
    cut = nodes // 2
    head, tail = total[:nodes], total[nodes:]

    def count(start):
        spot = start + rest
        return tail[:, spot : spot + 1] + LANES * tail[:, spot + 1 : spot + 2]

    low, high = count(0), count(HALF)
    low_safe, high_safe = jnp.maximum(low, 1.0), jnp.maximum(high, 1.0)
    head = jnp.concatenate([head[:cut] / low_safe, head[cut:] / high_safe], axis=0)
    lane = lane_index((cut, LANES))
    low_lane = lane < HALF
    spot = jnp.where(low_lane, lane, lane - HALF)
    touched = jnp.where(jnp.where(low_lane, low, high) > 0.5, 1.0, 0.0)
    tail = tail / jnp.where(low_lane, low_safe, high_safe)
    tail = jnp.where(spot < rest, tail, jnp.where(spot == rest, touched, 0.0))
    for part in range(out_ref.shape[0]):
        out_ref[part, 0:nodes, :] = head.astype(BF16)
        out_ref[part, nodes:, :] = tail.astype(BF16)


def pick_body(columns, column_ref, got_ref, out_ref):
    turns, asked, nodes = out_ref.shape
    peers = got_ref.shape[0]
    per_owner = asked // peers
    shift = lax.rem((columns - column_ref[0]) * per_owner, LANES)
    upright = lax.broadcasted_iota(jnp.int32, (per_owner, LANES), 0) == lane_index((per_owner, LANES))
    node_of = lane_index((per_owner, nodes))
    for peer in range(peers):
        named = pltpu.roll(got_ref[peer, WIRE:, :].astype(F32), shift, 1)
        for turn in range(turns):
            row = jnp.where(upright, named[turn : turn + 1, :], 0.0)
            row = jnp.sum(row, axis=1, keepdims=True).astype(jnp.int32)
            hits = jnp.where(row == node_of, 1.0, 0.0).astype(BF16)
            out_ref[turn, peer * per_owner : (peer + 1) * per_owner, :] = hits


def gates(rest, head, tail, head_w_ref, low_w_ref, high_w_ref, gate_ref, bias_ref):
    width = head_w_ref.shape[1]
    message = dot(head, head_w_ref[...]) + jnp.concatenate(
        [dot(tail, low_w_ref[...]), dot(tail, high_w_ref[...])], axis=0
    )
    touched = jnp.concatenate(
        [
            tail[:, rest : rest + 1].astype(F32),
            tail[:, HALF + rest : HALF + rest + 1].astype(F32),
        ],
        axis=0,
    )
    gate = dot(message.astype(BF16), gate_ref[...]) + bias_ref[...]
    update = jax.nn.sigmoid(gate[:, :width]) * jnp.where(touched > 0.5, 1.0, 0.0)
    return 1.0 - update, update * jnp.tanh(gate[:, width:])


def advance(rest, section, mean_ref, batches, memory_ref, weights):
    nodes = memory_ref.shape[0]
    state = memory_ref[...]
    for batch in range(batches):
        head, tail = mean_ref[batch, 0:nodes, :], mean_ref[batch, nodes:, :]
        decay, inject = gates(rest, head, tail, *weights)
        state = jnp.where(section > batch, decay * state + inject, state)
    return state


def before_body(rest, section_ref, mean_ref, memory_ref, *refs):
    weights, out_ref = refs[:-1], refs[-1]
    batches = mean_ref.shape[0] - 1
    before = advance(rest, section_ref[0], mean_ref, batches, memory_ref, weights).astype(BF16)
    for turn in range(out_ref.shape[0]):
        out_ref[turn] = before


def rows_body(pick_ref, table_ref, out_ref):
    turns, asked, nodes = pick_ref.shape
    peers, _, width = out_ref.shape
    per_owner = asked // peers
    for turn in range(turns):
        rows = dot(pick_ref[turn], table_ref[turn]).astype(BF16)
        spot = slice(turn * per_owner, (turn + 1) * per_owner)
        out_ref[:, spot, :] = rows.reshape(peers, per_owner, width)


def memory_body(rest, section_ref, mean_ref, memory_ref, *refs):
    weights, out_ref = refs[:-1], refs[-1]
    out_ref[...] = advance(rest, section_ref[0] + 1, mean_ref, mean_ref.shape[0], memory_ref, weights)


def event_body(*refs):
    sources, (scores_ref, grads_ref), targets = refs[:8], refs[8:10], refs[10:18]
    feat_ref, sems = refs[18:]
    rows_ref, ends_ref, near_ref, cos_ref, cot_ref, attn_ref, pred_ref, pred_out_ref = targets
    started = copies(sources, targets, sems)
    rows_copy, ends_copy, near_copy, cos_copy, cot_copy, attn_copy, pred_copy, out_copy = started
    for copy in (ends_copy, rows_copy, near_copy, cos_copy, attn_copy, cot_copy, out_copy, pred_copy):
        copy.start()
    ends_copy.wait()
    rows_copy.wait()
    slots, width = rows_ref.shape
    events = ends_ref.shape[1]
    pair = 2 * events
    near_count = near_ref.shape[0] // 2
    head_dim = width // HEADS
    diagonal = lax.broadcasted_iota(jnp.int32, (events, events), 0) == lane_index((events, events))

    def upright(index):
        index = jnp.where(diagonal, index.astype(F32), 0.0)
        return jnp.sum(index, axis=1, keepdims=True).astype(jnp.int32)

    def fetch(source, target):
        index = jnp.concatenate([upright(source), upright(target)], axis=0)
        lanes = lane_index((pair, slots))
        return dot(jnp.where(index == lanes, 1.0, 0.0).astype(BF16), rows_ref[...])

    own = fetch(ends_ref[0:1, :], ends_ref[1:2, :])
    near_copy.wait()
    for near in range(near_count):
        spot = slice(near * pair, (near + 1) * pair)
        other = near_count + near
        feat = fetch(near_ref[near : near + 1, :], near_ref[other : other + 1, :])
        if near == 0:
            cos_copy.wait()
        feat_ref[spot, :] = (feat + cos_ref[spot, :]).astype(BF16)
    attn_copy.wait()
    query = dot(own.astype(BF16), attn_ref[0]) * (1.0 / math.sqrt(head_dim))
    keys = dot(feat_ref[...], attn_ref[1])
    logits = [[] for _ in range(HEADS)]
    for near in range(near_count):
        match = query * keys[near * pair : (near + 1) * pair]
        for head in range(HEADS):
            part = match[:, head * head_dim : (head + 1) * head_dim]
            logits[head].append(jnp.sum(part, axis=1, keepdims=True))
    values = dot(feat_ref[...], attn_ref[2])
    mixed = []
    for head in range(HEADS):
        top = logits[head][0]
        for near in range(1, near_count):
            top = jnp.maximum(top, logits[head][near])
        powers = [jnp.exp(logit - top) for logit in logits[head]]
        total = powers[0]
        for near in range(1, near_count):
            total = total + powers[near]
        part = jnp.zeros((pair, head_dim), F32)
        for near in range(near_count):
            value = values[near * pair : (near + 1) * pair, head * head_dim : (head + 1) * head_dim]
            part = part + (powers[near] / total) * value
        mixed.append(part)
    mixed = jnp.concatenate(mixed, axis=1).astype(BF16)
    state = (own + dot(mixed, attn_ref[3])).astype(BF16)
    source, target = state[:events], state[events:]
    cot_copy.wait()
    out_copy.wait()
    pred_copy.wait()
    pre = dot(source, pred_ref[0]) + dot(target, pred_ref[1])
    gate = jax.nn.sigmoid(pre)
    pred_out = pred_out_ref[...]
    column = jnp.sum(pre * gate * pred_out, axis=1, keepdims=True)
    scores_ref[...] = jnp.sum(jnp.where(diagonal, column, 0.0), axis=0, keepdims=True)
    cot = jnp.sum(jnp.where(diagonal, cot_ref[...], 0.0), axis=1, keepdims=True)
    slope = (cot * pred_out * (gate * (1.0 + pre * (1.0 - gate)))).astype(BF16)
    back = jnp.concatenate([dot(slope, pred_ref[0], NT), dot(slope, pred_ref[1], NT)], axis=0)
    grads_ref[0:width, :] = dot(mixed, back.astype(BF16), TN).astype(BF16)
    grads_ref[width : 2 * width, :] = dot(source, slope, TN).astype(BF16)
    grads_ref[2 * width :, :] = dot(target, slope, TN).astype(BF16)


def grads_body(whole_ref, first_ref, rest_ref):
    width = first_ref.shape[0]
    whole = whole_ref[...].astype(F32).reshape(3 * width, width)
    first_ref[...] = whole[:width]
    for part in range(2):
        rest_ref[part] = whole[(part + 1) * width : (part + 2) * width]


def exchange(value, axis, groups=None):
    return lax.all_to_all(
        value, axis, split_axis=0, concat_axis=0, tiled=True, axis_index_groups=groups
    )


def sum_everywhere(grads, columns, rings):
    sections = lax.axis_size("tm")
    plane = [
        [
            (section * rings + ring) * columns + column
            for section in range(sections)
            for column in range(columns)
        ]
        for ring in range(rings)
    ]
    line = [[ring * columns + column for ring in range(rings)] for column in range(columns)]
    peers = len(plane[0])
    rows, width = grads.shape
    own = rows // peers
    pieces = exchange(grads.reshape(peers, own, width), ("tm", "dp"), plane)
    mine = jnp.sum(pieces.astype(F32), axis=0).astype(BF16)
    pieces = exchange(jnp.broadcast_to(mine[None], (rings, own, width)), "dp", line)
    mine = jnp.sum(pieces.astype(F32), axis=0).astype(BF16)
    whole = exchange(jnp.broadcast_to(mine[None], (peers, own, width)), ("tm", "dp"), plane)
    return dense_call(
        grads_body,
        (
            jax.ShapeDtypeStruct((width, width), F32),
            jax.ShapeDtypeStruct((rows // width - 1, width, width), F32),
        ),
        (whole,),
    )


def per_device(
    edge_feat,
    endpoint_slots,
    neighbor_slots,
    neighbor_gap,
    score_grad,
    node_list,
    memory0,
    msg_weight,
    gate_weight,
    gate_bias,
    omega,
    attn_weights,
    pred_weights,
    pred_out,
):
    groups = lax.axis_size("dp")
    batches = lax.axis_size("tm")
    nodes, width = memory0.shape
    list_len = node_list.shape[2]
    per_owner = list_len // groups
    features = edge_feat.shape[2]
    rest = features - LANES
    events = endpoint_slots.shape[2]
    near_count = neighbor_slots.shape[1] // 2
    columns = 4
    hops = 2
    rings = groups // columns
    turns = rings // hops
    peers = hops * columns
    line = [
        [(turn * hops + hop) * columns + column for turn in range(turns)]
        for column in range(columns)
        for hop in range(hops)
    ]
    across = [[turn * peers + peer for peer in range(peers)] for turn in range(turns)]
    place = lax.axis_index("dp").astype(jnp.int32)
    sent, named = pl.pallas_call(
        lambda *refs: pack_body(per_owner, *refs),
        out_shape=(
            jax.ShapeDtypeStruct((WIRE, LANES), BF16),
            jax.ShapeDtypeStruct((hops, turns, LANES), F32),
        ),
        in_specs=[pl.BlockSpec(memory_space=pltpu.HBM)] * 3,
        scratch_shapes=[
            pltpu.VMEM((HALF, LANES), F32),
            pltpu.VMEM((features, events), BF16),
            pltpu.VMEM((2, events), jnp.int32),
            pltpu.VMEM((1, list_len), jnp.int32),
            pltpu.SemaphoreType.DMA((3,)),
        ],
        compiler_params=ALONE,
    )(jnp.swapaxes(edge_feat[0], 0, 1), endpoint_slots[0], node_list[0])
    got = lax.all_gather(sent, "dp", axis=0, tiled=True, axis_index_groups=line)
    in_smem, in_vmem = pl.BlockSpec(memory_space=pltpu.SMEM), pl.BlockSpec(memory_space=pltpu.VMEM)
    sums = pl.pallas_call(
        lambda *refs: sums_body(rest, nodes, *refs),
        out_shape=jax.ShapeDtypeStruct((peers, WIRE + 2 * turns, LANES), BF16),
        in_specs=[in_smem, in_vmem, pl.BlockSpec(memory_space=pltpu.HBM)],
        scratch_shapes=[pltpu.VMEM((hops, turns, LANES), F32), pltpu.SemaphoreType.DMA],
        compiler_params=PARAMS,
    )(
        (place // peers)[None],
        got.reshape(turns, WIRE, LANES),
        pltpu.with_memory_space_constraint(named, pltpu.HBM),
    )
    got = exchange(sums, "dp", across)
    picks = pl.pallas_call(
        lambda *refs: pick_body(columns, *refs),
        out_shape=jax.ShapeDtypeStruct((turns, peers * per_owner, nodes), BF16),
        in_specs=[in_smem, in_vmem],
        compiler_params=PARAMS,
    )((place % columns)[None], got)
    pairs = 2 * near_count * events

    def by_neighbour(value):
        return jnp.swapaxes(value[0].reshape(2, near_count, events), 0, 1).reshape(pairs, 1)

    cosines = jnp.cos(by_neighbour(neighbor_gap).astype(F32) * omega[None, :])
    means = dense_call(
        lambda *refs: mean_body(rest, nodes, *refs),
        jax.ShapeDtypeStruct((batches, nodes + nodes // 2, LANES), BF16),
        (got,),
    )
    means = exchange(means, "tm")
    tail_w = jnp.pad(msg_weight[LANES:], ((0, HALF - rest), (0, 0)))
    section = lax.axis_index("tm").astype(jnp.int32)
    weights = (
        msg_weight[:LANES],
        jnp.pad(tail_w, ((0, HALF), (0, 0))),
        jnp.pad(tail_w, ((HALF, 0), (0, 0))),
        gate_weight,
        gate_bias[None],
    )

    def section_call(body, out_shape, args):
        return pl.pallas_call(
            lambda *refs: body(rest, *refs),
            out_shape=out_shape,
            in_specs=[pl.BlockSpec(memory_space=pltpu.SMEM)]
            + [pl.BlockSpec(memory_space=pltpu.VMEM)] * (len(args) + len(weights)),
            compiler_params=PARAMS,
        )(section[None], *args, *weights)

    before = section_call(
        before_body,
        jax.ShapeDtypeStruct((turns, nodes, width), BF16),
        (means, memory0),
    )
    table = exchange(before, "dp", line)
    new_memory = section_call(
        memory_body, jax.ShapeDtypeStruct((nodes, width), F32), (means, memory0)
    )
    def arrived(slot):
        owner, spot = slot // per_owner, slot % per_owner
        turn, peer = owner // peers, owner % peers
        return (peer * turns + turn) * per_owner + spot

    table, cosines, new_memory, end_spots, near_spots = lax.optimization_barrier(
        (table, cosines, new_memory, arrived(endpoint_slots[0]), arrived(neighbor_slots[0]))
    )
    rows = dense_call(
        rows_body,
        jax.ShapeDtypeStruct((peers, turns * per_owner, width), BF16),
        (picks, table),
    )
    slot_rows = exchange(rows, "dp", across).reshape(list_len, width)

    inputs = (
        slot_rows,
        end_spots,
        near_spots,
        cosines,
        score_grad,
        attn_weights,
        pred_weights,
        pred_out[None],
    )
    scores, grads = pl.pallas_call(
        event_body,
        out_shape=(
            jax.ShapeDtypeStruct((1, events), F32),
            jax.ShapeDtypeStruct((3 * width, width), BF16),
        ),
        in_specs=[pl.BlockSpec(memory_space=pltpu.HBM)] * len(inputs),
        scratch_shapes=[pltpu.VMEM(value.shape, value.dtype) for value in inputs]
        + [pltpu.VMEM((pairs, width), BF16), pltpu.SemaphoreType.DMA((len(inputs),))],
        compiler_params=ALONE,
    )(*inputs)
    grad_out, grad_pair = sum_everywhere(grads, columns, rings)
    return (scores, new_memory[None], grad_out, grad_pair)


def solution(mesh):
    in_specs = (
        P("tm", "dp", None),
        P("tm", None, "dp"),
        P("tm", None, "dp"),
        P("tm", None, "dp"),
        P("tm", "dp"),
        P("tm", "dp", None),
        P("dp", None),
        P(),
        P(),
        P(),
        P(),
        P(),
        P(),
        P(),
    )
    out_specs = (P("tm", "dp"), P("tm", "dp", None), P(), P())
    return jax.shard_map(
        per_device, mesh=mesh, in_specs=in_specs, out_specs=out_specs, check_vma=False
    )
```

```python
import math

import jax
import jax.numpy as jnp
from jax import lax
from jax.experimental import pallas as pl
from jax.experimental.pallas import tpu as pltpu
from jax.sharding import PartitionSpec as P

HEADS = 2
LANES = 128
HALF = LANES // 2
NT = (((1,), (1,)), ((), ()))
TN = (((0,), (0,)), ((), ()))
F32 = jnp.float32
BF16 = jnp.bfloat16
PARAMS = pltpu.CompilerParams(vmem_limit_bytes=12 * 1024 * 1024)
ALONE = pltpu.CompilerParams(vmem_limit_bytes=63 * 1024 * 1024)


def lane_index(shape):
    return lax.broadcasted_iota(jnp.int32, shape, len(shape) - 1)


def dot(left, right, dims=(((1,), (0,)), ((), ()))):
    return lax.dot_general(left, right, dims, preferred_element_type=F32)


def dense_call(body, out_shape, args, scratch=()):
    return pl.pallas_call(
        body,
        out_shape=out_shape,
        in_specs=[pl.BlockSpec(memory_space=pltpu.VMEM)] * len(args),
        scratch_shapes=list(scratch),
        compiler_params=PARAMS,
    )(*args)


def copies(sources, targets, sems):
    return [
        pltpu.make_async_copy(source, target, sems.at[index])
        for index, (source, target) in enumerate(zip(sources, targets))
    ]


def load(sources, targets, sems):
    started = copies(sources, targets, sems)
    for copy in started:
        copy.start()
    for copy in started:
        copy.wait()


WIRE = LANES + HALF


def pack_body(per_owner, feat_hbm, ends_hbm, list_hbm, out_ref, rows_ref, *refs):
    wide_ref, feat_ref, ends_ref, list_ref, sems = refs
    load((feat_hbm, ends_hbm, list_hbm), (feat_ref, ends_ref, list_ref), sems)
    rest = feat_ref.shape[0] - LANES
    hops = rows_ref.shape[0]
    slot_of = lax.broadcasted_iota(jnp.int32, (LANES, LANES), 0)
    diagonal = slot_of == lane_index((LANES, LANES))
    ends = ends_ref[...]
    found = [jnp.zeros((LANES, LANES), F32) for _ in range(2)]
    for block in range(list_ref.shape[1] // LANES):
        named = list_ref[0:1, block * LANES : (block + 1) * LANES].astype(F32)
        turn = block // hops
        rows_ref[block % hops, turn : turn + 1, :] = named
        named = jnp.sum(jnp.where(diagonal, named, 0.0), axis=1, keepdims=True)
        for side in range(2):
            hit = ends[side : side + 1, :] == slot_of + block * LANES
            found[side] = found[side] + jnp.where(hit, named, 0.0)
    wide_ref[...] = jnp.zeros_like(wide_ref)
    wide_ref[0:rest, :] = feat_ref[LANES:, :].astype(F32)
    wide_ref[rest : rest + 1, :] = jnp.ones((1, LANES), F32)
    for side in range(2):
        spot = rest + 1 + 2 * side
        wide_ref[spot : spot + 1, :] = (ends[side : side + 1, :] // per_owner).astype(F32)
        wide_ref[spot + 1 : spot + 2, :] = jnp.sum(found[side], axis=0, keepdims=True)
    out_ref[0:LANES, :] = feat_ref[0:LANES, :]
    out_ref[LANES:, :] = wide_ref[...].astype(BF16)


def sums_body(rest, nodes, turn_ref, got_ref, list_hbm, out_ref, list_ref, sem):
    copy = pltpu.make_async_copy(list_hbm, list_ref, sem)
    copy.start()
    turns = got_ref.shape[0]
    peers = out_ref.shape[0]
    hops = list_ref.shape[0]
    span = peers * nodes
    base = turn_ref[0] * span
    node_of = lax.broadcasted_iota(jnp.int32, (span, 2 * LANES), 0)
    total = jnp.zeros((span, 2 * LANES), F32)

    def keys(part, side):
        spot = rest + 1 + 2 * side
        rows = got_ref[part, LANES:, :].astype(F32)
        key = rows[spot : spot + 1, :] * nodes + rows[spot + 1 : spot + 2, :]
        return key.astype(jnp.int32) - base

    for part in range(0, turns, 2):
        hits = jnp.zeros((span, 2 * LANES), F32)
        for side in range(2):
            key = jnp.concatenate([keys(part, side), keys(part + 1, side)], axis=1)
            hits = hits + jnp.where(node_of == key, 1.0, 0.0)
        feats = []
        for source in (part, part + 1):
            tail = got_ref[source, LANES:, :]
            feats.append(jnp.concatenate([got_ref[source, 0:LANES, :], tail, tail], axis=0))
        total = total + dot(hits.astype(BF16), jnp.concatenate(feats, axis=1), NT)
    cut = nodes // 2
    lane = lane_index((cut, LANES))
    low_lane = lane < HALF
    spot = jnp.where(low_lane, lane, lane - HALF)
    copy.wait()
    for peer in range(peers):
        mine = total[peer * nodes : (peer + 1) * nodes]
        tail = jnp.where(low_lane, mine[:cut, LANES:], mine[cut:, LANES:])
        high = jnp.floor(tail * (1.0 / LANES))
        tail = jnp.where(spot == rest, tail - high * LANES, tail)
        tail = jnp.where(spot == rest + 1, pltpu.roll(high, 1, 1), tail)
        out_ref[peer, 0:LANES, :] = mine[:, :LANES].astype(BF16)
        out_ref[peer, LANES:WIRE, :] = tail.astype(BF16)
        named = list_ref[peer // (peers // hops)]
        out_ref[peer, WIRE:, :] = jnp.concatenate([named, named], axis=0).astype(BF16)


def mean_body(rest, nodes, got_ref, out_ref):
    total = got_ref[0, 0:WIRE, :].astype(F32)
    for column in range(1, got_ref.shape[0]):
        total = total + got_ref[column, 0:WIRE, :].astype(F32)
    cut = nodes // 2
    head, tail = total[:nodes], total[nodes:]

    def count(start):
        spot = start + rest
        return tail[:, spot : spot + 1] + LANES * tail[:, spot + 1 : spot + 2]

    low, high = count(0), count(HALF)
    low_safe, high_safe = jnp.maximum(low, 1.0), jnp.maximum(high, 1.0)
    head = jnp.concatenate([head[:cut] / low_safe, head[cut:] / high_safe], axis=0)
    lane = lane_index((cut, LANES))
    low_lane = lane < HALF
    spot = jnp.where(low_lane, lane, lane - HALF)
    touched = jnp.where(jnp.where(low_lane, low, high) > 0.5, 1.0, 0.0)
    tail = tail / jnp.where(low_lane, low_safe, high_safe)
    tail = jnp.where(spot < rest, tail, jnp.where(spot == rest, touched, 0.0))
    for part in range(out_ref.shape[0]):
        out_ref[part, 0:nodes, :] = head.astype(BF16)
        out_ref[part, nodes:, :] = tail.astype(BF16)


def pick_body(columns, column_ref, got_ref, out_ref):
    turns, asked, nodes = out_ref.shape
    peers = got_ref.shape[0]
    per_owner = asked // peers
    shift = lax.rem((columns - column_ref[0]) * per_owner, LANES)
    upright = lax.broadcasted_iota(jnp.int32, (per_owner, LANES), 0) == lane_index((per_owner, LANES))
    node_of = lane_index((per_owner, nodes))
    for peer in range(peers):
        named = pltpu.roll(got_ref[peer, WIRE:, :].astype(F32), shift, 1)
        for turn in range(turns):
            row = jnp.where(upright, named[turn : turn + 1, :], 0.0)
            row = jnp.sum(row, axis=1, keepdims=True).astype(jnp.int32)
            hits = jnp.where(row == node_of, 1.0, 0.0).astype(BF16)
            out_ref[turn, peer * per_owner : (peer + 1) * per_owner, :] = hits


def gates(rest, head, tail, head_w_ref, low_w_ref, high_w_ref, gate_ref, bias_ref):
    width = head_w_ref.shape[1]
    message = dot(head, head_w_ref[...]) + jnp.concatenate(
        [dot(tail, low_w_ref[...]), dot(tail, high_w_ref[...])], axis=0
    )
    touched = jnp.concatenate(
        [
            tail[:, rest : rest + 1].astype(F32),
            tail[:, HALF + rest : HALF + rest + 1].astype(F32),
        ],
        axis=0,
    )
    gate = dot(message.astype(BF16), gate_ref[...]) + bias_ref[...]
    update = jax.nn.sigmoid(gate[:, :width]) * jnp.where(touched > 0.5, 1.0, 0.0)
    return 1.0 - update, update * jnp.tanh(gate[:, width:])


def advance(rest, section, mean_ref, batches, memory_ref, weights):
    nodes = memory_ref.shape[0]
    state = memory_ref[...]
    for batch in range(batches):
        head, tail = mean_ref[batch, 0:nodes, :], mean_ref[batch, nodes:, :]
        decay, inject = gates(rest, head, tail, *weights)
        state = jnp.where(section > batch, decay * state + inject, state)
    return state


def before_body(rest, section_ref, mean_ref, memory_ref, *refs):
    weights, out_ref = refs[:-1], refs[-1]
    batches = mean_ref.shape[0] - 1
    before = advance(rest, section_ref[0], mean_ref, batches, memory_ref, weights)
    out_ref[...] = before.astype(BF16)


def rows_body(pick_ref, table_ref, out_ref):
    turns, asked, nodes = pick_ref.shape
    peers, _, width = out_ref.shape
    per_owner = asked // peers
    for turn in range(turns):
        rows = dot(pick_ref[turn], table_ref[turn]).astype(BF16)
        spot = slice(turn * per_owner, (turn + 1) * per_owner)
        out_ref[:, spot, :] = rows.reshape(peers, per_owner, width)


def memory_body(rest, section_ref, mean_ref, memory_ref, *refs):
    weights, out_ref = refs[:-1], refs[-1]
    out_ref[...] = advance(rest, section_ref[0] + 1, mean_ref, mean_ref.shape[0], memory_ref, weights)


def event_body(*refs):
    sources, (scores_ref, grads_ref), targets = refs[:9], refs[9:11], refs[11:20]
    feat_ref, sems = refs[20:]
    rows_ref, ends_ref, near_ref, early_ref, late_ref = targets[:5]
    cot_ref, attn_ref, pred_ref, pred_out_ref = targets[5:]
    started = copies(sources, targets, sems)
    rows_copy, ends_copy, near_copy, early_copy, late_copy = started[:5]
    cot_copy, attn_copy, pred_copy, out_copy = started[5:]
    for copy in (ends_copy, rows_copy, near_copy, early_copy, late_copy):
        copy.start()
    for copy in (attn_copy, cot_copy, out_copy, pred_copy):
        copy.start()
    ends_copy.wait()
    rows_copy.wait()
    slots, width = rows_ref.shape
    events = ends_ref.shape[1]
    pair = 2 * events
    near_count = near_ref.shape[0] // 2
    head_dim = width // HEADS
    diagonal = lax.broadcasted_iota(jnp.int32, (events, events), 0) == lane_index((events, events))

    def upright(index):
        index = jnp.where(diagonal, index.astype(F32), 0.0)
        return jnp.sum(index, axis=1, keepdims=True).astype(jnp.int32)

    def fetch(source, target):
        index = jnp.concatenate([upright(source), upright(target)], axis=0)
        lanes = lane_index((pair, slots))
        return dot(jnp.where(index == lanes, 1.0, 0.0).astype(BF16), rows_ref[...])

    own = fetch(ends_ref[0:1, :], ends_ref[1:2, :])
    near_copy.wait()
    for near in range(near_count):
        spot = slice(near * pair, (near + 1) * pair)
        other = near_count + near
        feat = fetch(near_ref[near : near + 1, :], near_ref[other : other + 1, :])
        half = near_count // 2
        if near == 0:
            early_copy.wait()
        if near == half:
            late_copy.wait()
        cos_ref = early_ref if near < half else late_ref
        cosines = cos_ref[near % half * pair : (near % half + 1) * pair, :]
        feat_ref[spot, :] = (feat + cosines).astype(BF16)
    attn_copy.wait()
    query = dot(own.astype(BF16), attn_ref[0]) * (1.0 / math.sqrt(head_dim))
    keys = dot(feat_ref[...], attn_ref[1])
    logits = [[] for _ in range(HEADS)]
    for near in range(near_count):
        match = query * keys[near * pair : (near + 1) * pair]
        for head in range(HEADS):
            part = match[:, head * head_dim : (head + 1) * head_dim]
            logits[head].append(jnp.sum(part, axis=1, keepdims=True))
    values = dot(feat_ref[...], attn_ref[2])
    mixed = []
    for head in range(HEADS):
        top = logits[head][0]
        for near in range(1, near_count):
            top = jnp.maximum(top, logits[head][near])
        powers = [jnp.exp(logit - top) for logit in logits[head]]
        total = powers[0]
        for near in range(1, near_count):
            total = total + powers[near]
        part = jnp.zeros((pair, head_dim), F32)
        for near in range(near_count):
            value = values[near * pair : (near + 1) * pair, head * head_dim : (head + 1) * head_dim]
            part = part + (powers[near] / total) * value
        mixed.append(part)
    mixed = jnp.concatenate(mixed, axis=1).astype(BF16)
    state = (own + dot(mixed, attn_ref[3])).astype(BF16)
    source, target = state[:events], state[events:]
    cot_copy.wait()
    out_copy.wait()
    pred_copy.wait()
    pre = dot(source, pred_ref[0]) + dot(target, pred_ref[1])
    gate = jax.nn.sigmoid(pre)
    pred_out = pred_out_ref[...]
    column = jnp.sum(pre * gate * pred_out, axis=1, keepdims=True)
    scores_ref[...] = jnp.sum(jnp.where(diagonal, column, 0.0), axis=0, keepdims=True)
    cot = jnp.sum(jnp.where(diagonal, cot_ref[...], 0.0), axis=1, keepdims=True)
    slope = (cot * pred_out * (gate * (1.0 + pre * (1.0 - gate)))).astype(BF16)
    back = jnp.concatenate([dot(slope, pred_ref[0], NT), dot(slope, pred_ref[1], NT)], axis=0)
    grads_ref[0:width, :] = dot(mixed, back.astype(BF16), TN).astype(BF16)
    grads_ref[width : 2 * width, :] = dot(source, slope, TN).astype(BF16)
    grads_ref[2 * width :, :] = dot(target, slope, TN).astype(BF16)


def grads_body(whole_ref, first_ref, rest_ref):
    width = first_ref.shape[0]
    whole = whole_ref[...].astype(F32).reshape(3 * width, width)
    first_ref[...] = whole[:width]
    for part in range(2):
        rest_ref[part] = whole[(part + 1) * width : (part + 2) * width]


def exchange(value, axis, groups=None):
    return lax.all_to_all(
        value, axis, split_axis=0, concat_axis=0, tiled=True, axis_index_groups=groups
    )


def sum_everywhere(grads, columns, rings):
    sections = lax.axis_size("tm")
    plane = [
        [
            (section * rings + ring) * columns + column
            for section in range(sections)
            for column in range(columns)
        ]
        for ring in range(rings)
    ]
    line = [[ring * columns + column for ring in range(rings)] for column in range(columns)]
    peers = len(plane[0])
    rows, width = grads.shape
    own = rows // peers
    pieces = exchange(grads.reshape(peers, own, width), ("tm", "dp"), plane)
    mine = jnp.sum(pieces.astype(F32), axis=0).astype(BF16)
    pieces = exchange(jnp.broadcast_to(mine[None], (rings, own, width)), "dp", line)
    mine = jnp.sum(pieces.astype(F32), axis=0).astype(BF16)
    whole = exchange(jnp.broadcast_to(mine[None], (peers, own, width)), ("tm", "dp"), plane)
    return dense_call(
        grads_body,
        (
            jax.ShapeDtypeStruct((width, width), F32),
            jax.ShapeDtypeStruct((rows // width - 1, width, width), F32),
        ),
        (whole,),
    )


def per_device(
    edge_feat,
    endpoint_slots,
    neighbor_slots,
    neighbor_gap,
    score_grad,
    node_list,
    memory0,
    msg_weight,
    gate_weight,
    gate_bias,
    omega,
    attn_weights,
    pred_weights,
    pred_out,
):
    groups = lax.axis_size("dp")
    batches = lax.axis_size("tm")
    nodes, width = memory0.shape
    list_len = node_list.shape[2]
    per_owner = list_len // groups
    features = edge_feat.shape[2]
    rest = features - LANES
    events = endpoint_slots.shape[2]
    near_count = neighbor_slots.shape[1] // 2
    columns = 4
    hops = 2
    rings = groups // columns
    turns = rings // hops
    peers = hops * columns
    line = [
        [(turn * hops + hop) * columns + column for turn in range(turns)]
        for column in range(columns)
        for hop in range(hops)
    ]
    across = [[turn * peers + peer for peer in range(peers)] for turn in range(turns)]
    place = lax.axis_index("dp").astype(jnp.int32)
    sent, named = pl.pallas_call(
        lambda *refs: pack_body(per_owner, *refs),
        out_shape=(
            jax.ShapeDtypeStruct((WIRE, LANES), BF16),
            jax.ShapeDtypeStruct((hops, turns, LANES), F32),
        ),
        in_specs=[pl.BlockSpec(memory_space=pltpu.HBM)] * 3,
        scratch_shapes=[
            pltpu.VMEM((HALF, LANES), F32),
            pltpu.VMEM((features, events), BF16),
            pltpu.VMEM((2, events), jnp.int32),
            pltpu.VMEM((1, list_len), jnp.int32),
            pltpu.SemaphoreType.DMA((3,)),
        ],
        compiler_params=ALONE,
    )(jnp.swapaxes(edge_feat[0], 0, 1), endpoint_slots[0], node_list[0])
    got = lax.all_gather(sent, "dp", axis=0, tiled=True, axis_index_groups=line)
    in_smem, in_vmem = pl.BlockSpec(memory_space=pltpu.SMEM), pl.BlockSpec(memory_space=pltpu.VMEM)
    sums = pl.pallas_call(
        lambda *refs: sums_body(rest, nodes, *refs),
        out_shape=jax.ShapeDtypeStruct((peers, WIRE + 2 * turns, LANES), BF16),
        in_specs=[in_smem, in_vmem, pl.BlockSpec(memory_space=pltpu.HBM)],
        scratch_shapes=[pltpu.VMEM((hops, turns, LANES), F32), pltpu.SemaphoreType.DMA],
        compiler_params=PARAMS,
    )(
        (place // peers)[None],
        got.reshape(turns, WIRE, LANES),
        pltpu.with_memory_space_constraint(named, pltpu.HBM),
    )
    got = exchange(sums, "dp", across)
    picks = pl.pallas_call(
        lambda *refs: pick_body(columns, *refs),
        out_shape=jax.ShapeDtypeStruct((turns, peers * per_owner, nodes), BF16),
        in_specs=[in_smem, in_vmem],
        compiler_params=PARAMS,
    )((place % columns)[None], got)
    pairs = 2 * near_count * events

    def by_neighbour(value):
        return jnp.swapaxes(value[0].reshape(2, near_count, events), 0, 1).reshape(pairs, 1)

    gaps = by_neighbour(neighbor_gap).astype(F32)
    cut = pairs // 2
    early = jnp.cos(gaps[:cut] * omega[None, :])
    means = dense_call(
        lambda *refs: mean_body(rest, nodes, *refs),
        jax.ShapeDtypeStruct((batches, nodes + nodes // 2, LANES), BF16),
        (got,),
    )
    def arrived(slot):
        owner, spot = slot // per_owner, slot % per_owner
        turn, peer = owner // peers, owner % peers
        return (peer * turns + turn) * per_owner + spot

    means, picks, early, end_spots, near_spots = lax.optimization_barrier(
        (
            exchange(means, "tm"),
            picks,
            early,
            arrived(endpoint_slots[0]),
            arrived(neighbor_slots[0]),
        )
    )
    tail_w = jnp.pad(msg_weight[LANES:], ((0, HALF - rest), (0, 0)))
    section = lax.axis_index("tm").astype(jnp.int32)
    weights = (
        msg_weight[:LANES],
        jnp.pad(tail_w, ((0, HALF), (0, 0))),
        jnp.pad(tail_w, ((HALF, 0), (0, 0))),
        gate_weight,
        gate_bias[None],
    )

    def section_call(body, out_shape, args):
        return pl.pallas_call(
            lambda *refs: body(rest, *refs),
            out_shape=out_shape,
            in_specs=[pl.BlockSpec(memory_space=pltpu.SMEM)]
            + [pl.BlockSpec(memory_space=pltpu.VMEM)] * (len(args) + len(weights)),
            compiler_params=PARAMS,
        )(section[None], *args, *weights)

    before = section_call(
        before_body,
        jax.ShapeDtypeStruct((nodes, width), BF16),
        (means, memory0),
    )
    table = lax.all_gather(before, "dp", axis=0, tiled=True, axis_index_groups=line)
    table = table.reshape(turns, nodes, width)
    new_memory = section_call(
        memory_body, jax.ShapeDtypeStruct((nodes, width), F32), (means, memory0)
    )
    rows = dense_call(
        rows_body,
        jax.ShapeDtypeStruct((peers, turns * per_owner, width), BF16),
        (picks, table),
    )
    rows, omega_late = lax.optimization_barrier((rows, omega))
    slot_rows = exchange(rows, "dp", across).reshape(list_len, width)
    late = jnp.cos(gaps[cut:] * omega_late[None, :])
    late, new_memory = lax.optimization_barrier((late, new_memory))

    inputs = (
        slot_rows,
        end_spots,
        near_spots,
        early,
        late,
        score_grad,
        attn_weights,
        pred_weights,
        pred_out[None],
    )
    scores, grads = pl.pallas_call(
        event_body,
        out_shape=(
            jax.ShapeDtypeStruct((1, events), F32),
            jax.ShapeDtypeStruct((3 * width, width), BF16),
        ),
        in_specs=[pl.BlockSpec(memory_space=pltpu.HBM)] * len(inputs),
        scratch_shapes=[pltpu.VMEM(value.shape, value.dtype) for value in inputs]
        + [pltpu.VMEM((pairs, width), BF16), pltpu.SemaphoreType.DMA((len(inputs),))],
        compiler_params=ALONE,
    )(*inputs)
    grad_out, grad_pair = sum_everywhere(grads, columns, rings)
    return (scores, new_memory[None], grad_out, grad_pair)


def solution(mesh):
    in_specs = (
        P("tm", "dp", None),
        P("tm", None, "dp"),
        P("tm", None, "dp"),
        P("tm", None, "dp"),
        P("tm", "dp"),
        P("tm", "dp", None),
        P("dp", None),
        P(),
        P(),
        P(),
        P(),
        P(),
        P(),
        P(),
    )
    out_specs = (P("tm", "dp"), P("tm", "dp", None), P(), P())
    return jax.shard_map(
        per_device, mesh=mesh, in_specs=in_specs, out_specs=out_specs, check_vma=False
    )
```

```python
import math

import jax
import jax.numpy as jnp
from jax import lax
from jax.experimental import pallas as pl
from jax.experimental.pallas import tpu as pltpu
from jax.sharding import PartitionSpec as P

HEADS = 2
LANES = 128
HALF = LANES // 2
NT = (((1,), (1,)), ((), ()))
TN = (((0,), (0,)), ((), ()))
F32 = jnp.float32
BF16 = jnp.bfloat16
PARAMS = pltpu.CompilerParams(vmem_limit_bytes=12 * 1024 * 1024)
ALONE = pltpu.CompilerParams(vmem_limit_bytes=63 * 1024 * 1024)


def lane_index(shape):
    return lax.broadcasted_iota(jnp.int32, shape, len(shape) - 1)


def dot(left, right, dims=(((1,), (0,)), ((), ()))):
    return lax.dot_general(left, right, dims, preferred_element_type=F32)


def dense_call(body, out_shape, args, scratch=()):
    return pl.pallas_call(
        body,
        out_shape=out_shape,
        in_specs=[pl.BlockSpec(memory_space=pltpu.VMEM)] * len(args),
        scratch_shapes=list(scratch),
        compiler_params=PARAMS,
    )(*args)


def copies(sources, targets, sems):
    return [
        pltpu.make_async_copy(source, target, sems.at[index])
        for index, (source, target) in enumerate(zip(sources, targets))
    ]


def load(sources, targets, sems):
    started = copies(sources, targets, sems)
    for copy in started:
        copy.start()
    for copy in started:
        copy.wait()


WIRE = LANES + HALF


def pack_body(per_owner, feat_hbm, ends_hbm, list_hbm, out_ref, rows_ref, *refs):
    wide_ref, feat_ref, ends_ref, list_ref, sems = refs
    load((feat_hbm, ends_hbm, list_hbm), (feat_ref, ends_ref, list_ref), sems)
    rest = feat_ref.shape[0] - LANES
    hops = rows_ref.shape[0]
    slot_of = lax.broadcasted_iota(jnp.int32, (LANES, LANES), 0)
    diagonal = slot_of == lane_index((LANES, LANES))
    ends = ends_ref[...]
    found = [jnp.zeros((LANES, LANES), F32) for _ in range(2)]
    for block in range(list_ref.shape[1] // LANES):
        named = list_ref[0:1, block * LANES : (block + 1) * LANES].astype(F32)
        turn = block // hops
        rows_ref[block % hops, turn : turn + 1, :] = named
        named = jnp.sum(jnp.where(diagonal, named, 0.0), axis=1, keepdims=True)
        for side in range(2):
            hit = ends[side : side + 1, :] == slot_of + block * LANES
            found[side] = found[side] + jnp.where(hit, named, 0.0)
    wide_ref[...] = jnp.zeros_like(wide_ref)
    wide_ref[0:rest, :] = feat_ref[LANES:, :].astype(F32)
    wide_ref[rest : rest + 1, :] = jnp.ones((1, LANES), F32)
    for side in range(2):
        spot = rest + 1 + 2 * side
        wide_ref[spot : spot + 1, :] = (ends[side : side + 1, :] // per_owner).astype(F32)
        wide_ref[spot + 1 : spot + 2, :] = jnp.sum(found[side], axis=0, keepdims=True)
    out_ref[0:LANES, :] = feat_ref[0:LANES, :]
    out_ref[LANES:, :] = wide_ref[...].astype(BF16)


def sums_body(rest, nodes, turn_ref, got_ref, list_hbm, out_ref, list_ref, sem):
    copy = pltpu.make_async_copy(list_hbm, list_ref, sem)
    copy.start()
    turns = got_ref.shape[0]
    peers = out_ref.shape[0]
    hops = list_ref.shape[0]
    span = peers * nodes
    base = turn_ref[0] * span
    node_of = lax.broadcasted_iota(jnp.int32, (span, 2 * LANES), 0)
    total = jnp.zeros((span, 2 * LANES), F32)

    def keys(part, side):
        spot = rest + 1 + 2 * side
        rows = got_ref[part, LANES:, :].astype(F32)
        key = rows[spot : spot + 1, :] * nodes + rows[spot + 1 : spot + 2, :]
        return key.astype(jnp.int32) - base

    for part in range(0, turns, 2):
        hits = jnp.zeros((span, 2 * LANES), F32)
        for side in range(2):
            key = jnp.concatenate([keys(part, side), keys(part + 1, side)], axis=1)
            hits = hits + jnp.where(node_of == key, 1.0, 0.0)
        feats = []
        for source in (part, part + 1):
            tail = got_ref[source, LANES:, :]
            feats.append(jnp.concatenate([got_ref[source, 0:LANES, :], tail, tail], axis=0))
        total = total + dot(hits.astype(BF16), jnp.concatenate(feats, axis=1), NT)
    cut = nodes // 2
    lane = lane_index((cut, LANES))
    low_lane = lane < HALF
    spot = jnp.where(low_lane, lane, lane - HALF)
    copy.wait()
    for peer in range(peers):
        mine = total[peer * nodes : (peer + 1) * nodes]
        tail = jnp.where(low_lane, mine[:cut, LANES:], mine[cut:, LANES:])
        high = jnp.floor(tail * (1.0 / LANES))
        tail = jnp.where(spot == rest, tail - high * LANES, tail)
        tail = jnp.where(spot == rest + 1, pltpu.roll(high, 1, 1), tail)
        out_ref[peer, 0:LANES, :] = mine[:, :LANES].astype(BF16)
        out_ref[peer, LANES:WIRE, :] = tail.astype(BF16)
        named = list_ref[peer // (peers // hops)]
        out_ref[peer, WIRE:, :] = jnp.concatenate([named, named], axis=0).astype(BF16)


def mean_body(rest, nodes, got_ref, out_ref):
    total = got_ref[0, 0:WIRE, :].astype(F32)
    for column in range(1, got_ref.shape[0]):
        total = total + got_ref[column, 0:WIRE, :].astype(F32)
    cut = nodes // 2
    head, tail = total[:nodes], total[nodes:]

    def count(start):
        spot = start + rest
        return tail[:, spot : spot + 1] + LANES * tail[:, spot + 1 : spot + 2]

    low, high = count(0), count(HALF)
    low_safe, high_safe = jnp.maximum(low, 1.0), jnp.maximum(high, 1.0)
    head = jnp.concatenate([head[:cut] / low_safe, head[cut:] / high_safe], axis=0)
    lane = lane_index((cut, LANES))
    low_lane = lane < HALF
    spot = jnp.where(low_lane, lane, lane - HALF)
    touched = jnp.where(jnp.where(low_lane, low, high) > 0.5, 1.0, 0.0)
    tail = tail / jnp.where(low_lane, low_safe, high_safe)
    tail = jnp.where(spot < rest, tail, jnp.where(spot == rest, touched, 0.0))
    for part in range(out_ref.shape[0]):
        out_ref[part, 0:nodes, :] = head.astype(BF16)
        out_ref[part, nodes:, :] = tail.astype(BF16)


def pick_body(columns, column_ref, got_ref, out_ref):
    turns, asked, nodes = out_ref.shape
    peers = got_ref.shape[0]
    per_owner = asked // peers
    shift = lax.rem((columns - column_ref[0]) * per_owner, LANES)
    upright = lax.broadcasted_iota(jnp.int32, (per_owner, LANES), 0) == lane_index((per_owner, LANES))
    node_of = lane_index((per_owner, nodes))
    for peer in range(peers):
        named = pltpu.roll(got_ref[peer, WIRE:, :].astype(F32), shift, 1)
        for turn in range(turns):
            row = jnp.where(upright, named[turn : turn + 1, :], 0.0)
            row = jnp.sum(row, axis=1, keepdims=True).astype(jnp.int32)
            hits = jnp.where(row == node_of, 1.0, 0.0).astype(BF16)
            out_ref[turn, peer * per_owner : (peer + 1) * per_owner, :] = hits


def gates(rest, head, tail, head_w_ref, low_w_ref, high_w_ref, gate_ref, bias_ref):
    width = head_w_ref.shape[1]
    message = dot(head, head_w_ref[...]) + jnp.concatenate(
        [dot(tail, low_w_ref[...]), dot(tail, high_w_ref[...])], axis=0
    )
    touched = jnp.concatenate(
        [
            tail[:, rest : rest + 1].astype(F32),
            tail[:, HALF + rest : HALF + rest + 1].astype(F32),
        ],
        axis=0,
    )
    gate = dot(message.astype(BF16), gate_ref[...]) + bias_ref[...]
    update = jax.nn.sigmoid(gate[:, :width]) * jnp.where(touched > 0.5, 1.0, 0.0)
    return 1.0 - update, update * jnp.tanh(gate[:, width:])


def advance(rest, section, mean_ref, batches, memory_ref, weights):
    nodes = memory_ref.shape[0]
    state = memory_ref[...]
    for batch in range(batches):
        head, tail = mean_ref[batch, 0:nodes, :], mean_ref[batch, nodes:, :]
        decay, inject = gates(rest, head, tail, *weights)
        state = jnp.where(section > batch, decay * state + inject, state)
    return state


def before_body(rest, section_ref, mean_ref, memory_ref, *refs):
    weights, out_ref = refs[:-1], refs[-1]
    batches = mean_ref.shape[0] - 1
    before = advance(rest, section_ref[0], mean_ref, batches, memory_ref, weights)
    out_ref[...] = before.astype(BF16)


def rows_body(pick_ref, table_ref, out_ref):
    turns, asked, nodes = pick_ref.shape
    peers, _, width = out_ref.shape
    per_owner = asked // peers
    for turn in range(turns):
        rows = dot(pick_ref[turn], table_ref[turn]).astype(BF16)
        spot = slice(turn * per_owner, (turn + 1) * per_owner)
        out_ref[:, spot, :] = rows.reshape(peers, per_owner, width)


def memory_body(rest, section_ref, mean_ref, memory_ref, *refs):
    weights, out_ref = refs[:-1], refs[-1]
    out_ref[...] = advance(rest, section_ref[0] + 1, mean_ref, mean_ref.shape[0], memory_ref, weights)


def event_body(*refs):
    sources, (scores_ref, grads_ref), targets = refs[:9], refs[9:11], refs[11:20]
    feat_ref, sems = refs[20:]
    rows_ref, ends_ref, near_ref, early_ref, late_ref = targets[:5]
    cot_ref, attn_ref, pred_ref, pred_out_ref = targets[5:]
    started = copies(sources, targets, sems)
    rows_copy, ends_copy, near_copy, early_copy, late_copy = started[:5]
    cot_copy, attn_copy, pred_copy, out_copy = started[5:]
    for copy in (ends_copy, rows_copy, near_copy):
        copy.start()
    ends_copy.wait()
    rows_copy.wait()
    for copy in (early_copy, attn_copy, late_copy, cot_copy, out_copy, pred_copy):
        copy.start()
    slots, width = rows_ref.shape
    events = ends_ref.shape[1]
    pair = 2 * events
    near_count = near_ref.shape[0] // 2
    head_dim = width // HEADS
    diagonal = lax.broadcasted_iota(jnp.int32, (events, events), 0) == lane_index((events, events))

    def upright(index):
        index = jnp.where(diagonal, index.astype(F32), 0.0)
        return jnp.sum(index, axis=1, keepdims=True).astype(jnp.int32)

    def fetch(source, target):
        index = jnp.concatenate([upright(source), upright(target)], axis=0)
        lanes = lane_index((pair, slots))
        return dot(jnp.where(index == lanes, 1.0, 0.0).astype(BF16), rows_ref[...])

    own = fetch(ends_ref[0:1, :], ends_ref[1:2, :])
    near_copy.wait()
    for near in range(near_count):
        spot = slice(near * pair, (near + 1) * pair)
        other = near_count + near
        feat = fetch(near_ref[near : near + 1, :], near_ref[other : other + 1, :])
        half = near_count // 2
        if near == 0:
            early_copy.wait()
        if near == half:
            late_copy.wait()
        cos_ref = early_ref if near < half else late_ref
        cosines = cos_ref[near % half * pair : (near % half + 1) * pair, :]
        feat_ref[spot, :] = (feat + cosines).astype(BF16)
    attn_copy.wait()
    query = dot(own.astype(BF16), attn_ref[0]) * (1.0 / math.sqrt(head_dim))
    keys = dot(feat_ref[...], attn_ref[1])
    logits = [[] for _ in range(HEADS)]
    for near in range(near_count):
        match = query * keys[near * pair : (near + 1) * pair]
        for head in range(HEADS):
            part = match[:, head * head_dim : (head + 1) * head_dim]
            logits[head].append(jnp.sum(part, axis=1, keepdims=True))
    values = dot(feat_ref[...], attn_ref[2])
    mixed = []
    for head in range(HEADS):
        top = logits[head][0]
        for near in range(1, near_count):
            top = jnp.maximum(top, logits[head][near])
        powers = [jnp.exp(logit - top) for logit in logits[head]]
        total = powers[0]
        for near in range(1, near_count):
            total = total + powers[near]
        part = jnp.zeros((pair, head_dim), F32)
        for near in range(near_count):
            value = values[near * pair : (near + 1) * pair, head * head_dim : (head + 1) * head_dim]
            part = part + (powers[near] / total) * value
        mixed.append(part)
    mixed = jnp.concatenate(mixed, axis=1).astype(BF16)
    state = (own + dot(mixed, attn_ref[3])).astype(BF16)
    source, target = state[:events], state[events:]
    cot_copy.wait()
    out_copy.wait()
    pred_copy.wait()
    pre = dot(source, pred_ref[0]) + dot(target, pred_ref[1])
    gate = jax.nn.sigmoid(pre)
    pred_out = pred_out_ref[...]
    column = jnp.sum(pre * gate * pred_out, axis=1, keepdims=True)
    scores_ref[...] = jnp.sum(jnp.where(diagonal, column, 0.0), axis=0, keepdims=True)
    cot = jnp.sum(jnp.where(diagonal, cot_ref[...], 0.0), axis=1, keepdims=True)
    slope = (cot * pred_out * (gate * (1.0 + pre * (1.0 - gate)))).astype(BF16)
    back = jnp.concatenate([dot(slope, pred_ref[0], NT), dot(slope, pred_ref[1], NT)], axis=0)
    halves = width // LANES
    for index, (left, right) in enumerate(
        ((mixed, back.astype(BF16)), (source, slope), (target, slope))
    ):
        grad = dot(left, right, TN).astype(BF16)
        for half in range(halves):
            start = (index * halves + half) * width
            grads_ref[start : start + width, :] = grad[:, half * LANES : (half + 1) * LANES]


def grads_body(whole_ref, first_ref, rest_ref):
    width = first_ref.shape[0]
    halves = width // LANES
    whole = whole_ref[...].astype(F32).reshape(3 * halves * width, LANES)
    for half in range(halves):
        spot = slice(half * LANES, (half + 1) * LANES)
        first_ref[:, spot] = whole[half * width : (half + 1) * width]
        for part in range(2):
            start = ((part + 1) * halves + half) * width
            rest_ref[part, :, spot] = whole[start : start + width]


def exchange(value, axis, groups=None):
    return lax.all_to_all(
        value, axis, split_axis=0, concat_axis=0, tiled=True, axis_index_groups=groups
    )


def sum_everywhere(grads, line, peers, width):
    sections = lax.axis_size("tm")
    turns = len(line[0])
    near = [
        [(section * turns + turn) * peers + peer for section in range(sections) for peer in range(peers)]
        for turn in range(turns)
    ]
    group = len(near[0])
    own = grads.shape[0] // group
    pieces = exchange(grads.reshape(group, own, LANES), ("tm", "dp"), near)
    mine = jnp.sum(pieces.astype(F32), axis=0).astype(BF16)
    pieces = exchange(jnp.broadcast_to(mine[None], (turns, own, LANES)), "dp", line)
    mine = jnp.sum(pieces.astype(F32), axis=0).astype(BF16)
    whole = exchange(jnp.broadcast_to(mine[None], (group, own, LANES)), ("tm", "dp"), near)
    return dense_call(
        grads_body,
        (
            jax.ShapeDtypeStruct((width, width), F32),
            jax.ShapeDtypeStruct((2, width, width), F32),
        ),
        (whole,),
    )


def per_device(
    edge_feat,
    endpoint_slots,
    neighbor_slots,
    neighbor_gap,
    score_grad,
    node_list,
    memory0,
    msg_weight,
    gate_weight,
    gate_bias,
    omega,
    attn_weights,
    pred_weights,
    pred_out,
):
    groups = lax.axis_size("dp")
    batches = lax.axis_size("tm")
    nodes, width = memory0.shape
    list_len = node_list.shape[2]
    per_owner = list_len // groups
    features = edge_feat.shape[2]
    rest = features - LANES
    events = endpoint_slots.shape[2]
    near_count = neighbor_slots.shape[1] // 2
    columns = 4
    hops = 2
    rings = groups // columns
    turns = rings // hops
    peers = hops * columns
    line = [
        [(turn * hops + hop) * columns + column for turn in range(turns)]
        for column in range(columns)
        for hop in range(hops)
    ]
    across = [[turn * peers + peer for peer in range(peers)] for turn in range(turns)]
    place = lax.axis_index("dp").astype(jnp.int32)
    sent, named = pl.pallas_call(
        lambda *refs: pack_body(per_owner, *refs),
        out_shape=(
            jax.ShapeDtypeStruct((WIRE, LANES), BF16),
            jax.ShapeDtypeStruct((hops, turns, LANES), F32),
        ),
        in_specs=[pl.BlockSpec(memory_space=pltpu.HBM)] * 3,
        scratch_shapes=[
            pltpu.VMEM((HALF, LANES), F32),
            pltpu.VMEM((features, events), BF16),
            pltpu.VMEM((2, events), jnp.int32),
            pltpu.VMEM((1, list_len), jnp.int32),
            pltpu.SemaphoreType.DMA((3,)),
        ],
        compiler_params=ALONE,
    )(jnp.swapaxes(edge_feat[0], 0, 1), endpoint_slots[0], node_list[0])
    got = lax.all_gather(sent, "dp", axis=0, tiled=True, axis_index_groups=line)
    in_smem, in_vmem = pl.BlockSpec(memory_space=pltpu.SMEM), pl.BlockSpec(memory_space=pltpu.VMEM)
    sums = pl.pallas_call(
        lambda *refs: sums_body(rest, nodes, *refs),
        out_shape=jax.ShapeDtypeStruct((peers, WIRE + 2 * turns, LANES), BF16),
        in_specs=[in_smem, in_vmem, pl.BlockSpec(memory_space=pltpu.HBM)],
        scratch_shapes=[pltpu.VMEM((hops, turns, LANES), F32), pltpu.SemaphoreType.DMA],
        compiler_params=PARAMS,
    )(
        (place // peers)[None],
        got.reshape(turns, WIRE, LANES),
        pltpu.with_memory_space_constraint(named, pltpu.HBM),
    )
    got = exchange(sums, "dp", across)
    picks = pl.pallas_call(
        lambda *refs: pick_body(columns, *refs),
        out_shape=jax.ShapeDtypeStruct((turns, peers * per_owner, nodes), BF16),
        in_specs=[in_smem, in_vmem],
        compiler_params=PARAMS,
    )((place % columns)[None], got)
    pairs = 2 * near_count * events

    def by_neighbour(value):
        return jnp.swapaxes(value[0].reshape(2, near_count, events), 0, 1).reshape(pairs, 1)

    gaps = by_neighbour(neighbor_gap).astype(F32)
    cut = pairs // 2
    early = jnp.cos(gaps[:cut] * omega[None, :])
    means = dense_call(
        lambda *refs: mean_body(rest, nodes, *refs),
        jax.ShapeDtypeStruct((batches, nodes + nodes // 2, LANES), BF16),
        (got,),
    )
    def arrived(slot):
        owner, spot = slot // per_owner, slot % per_owner
        turn, peer = owner // peers, owner % peers
        return (peer * turns + turn) * per_owner + spot

    means, picks, early, end_spots, near_spots = lax.optimization_barrier(
        (
            exchange(means, "tm"),
            picks,
            early,
            arrived(endpoint_slots[0]),
            arrived(neighbor_slots[0]),
        )
    )
    tail_w = jnp.pad(msg_weight[LANES:], ((0, HALF - rest), (0, 0)))
    section = lax.axis_index("tm").astype(jnp.int32)
    weights = (
        msg_weight[:LANES],
        jnp.pad(tail_w, ((0, HALF), (0, 0))),
        jnp.pad(tail_w, ((HALF, 0), (0, 0))),
        gate_weight,
        gate_bias[None],
    )

    def section_call(body, out_shape, args):
        return pl.pallas_call(
            lambda *refs: body(rest, *refs),
            out_shape=out_shape,
            in_specs=[pl.BlockSpec(memory_space=pltpu.SMEM)]
            + [pl.BlockSpec(memory_space=pltpu.VMEM)] * (len(args) + len(weights)),
            compiler_params=PARAMS,
        )(section[None], *args, *weights)

    before = section_call(
        before_body,
        jax.ShapeDtypeStruct((nodes, width), BF16),
        (means, memory0),
    )
    table = lax.all_gather(before, "dp", axis=0, tiled=True, axis_index_groups=line)
    table = table.reshape(turns, nodes, width)
    new_memory = section_call(
        memory_body, jax.ShapeDtypeStruct((nodes, width), F32), (means, memory0)
    )
    rows = dense_call(
        rows_body,
        jax.ShapeDtypeStruct((peers, turns * per_owner, width), BF16),
        (picks, table),
    )
    rows, omega_late = lax.optimization_barrier((rows, omega))
    slot_rows = exchange(rows, "dp", across).reshape(list_len, width)
    late = jnp.cos(gaps[cut:] * omega_late[None, :])
    late, new_memory = lax.optimization_barrier((late, new_memory))

    inputs = (
        slot_rows,
        end_spots,
        near_spots,
        early,
        late,
        score_grad,
        attn_weights,
        pred_weights,
        pred_out[None],
    )
    scores, grads = pl.pallas_call(
        event_body,
        out_shape=(
            jax.ShapeDtypeStruct((1, events), F32),
            jax.ShapeDtypeStruct((3 * width * width // LANES, LANES), BF16),
        ),
        in_specs=[pl.BlockSpec(memory_space=pltpu.HBM)] * len(inputs),
        scratch_shapes=[pltpu.VMEM(value.shape, value.dtype) for value in inputs]
        + [pltpu.VMEM((pairs, width), BF16), pltpu.SemaphoreType.DMA((len(inputs),))],
        compiler_params=ALONE,
    )(*inputs)
    grad_out, grad_pair = sum_everywhere(grads, line, peers, width)
    return (scores, new_memory[None], grad_out, grad_pair)


def solution(mesh):
    in_specs = (
        P("tm", "dp", None),
        P("tm", None, "dp"),
        P("tm", None, "dp"),
        P("tm", None, "dp"),
        P("tm", "dp"),
        P("tm", "dp", None),
        P("dp", None),
        P(),
        P(),
        P(),
        P(),
        P(),
        P(),
        P(),
    )
    out_specs = (P("tm", "dp"), P("tm", "dp", None), P(), P())
    return jax.shard_map(
        per_device, mesh=mesh, in_specs=in_specs, out_specs=out_specs, check_vma=False
    )
```

```python
import math

import jax
import jax.numpy as jnp
from jax import lax
from jax.experimental import pallas as pl
from jax.experimental.pallas import tpu as pltpu
from jax.sharding import PartitionSpec as P

HEADS = 2
LANES = 128
HALF = LANES // 2
NT = (((1,), (1,)), ((), ()))
TN = (((0,), (0,)), ((), ()))
F32 = jnp.float32
BF16 = jnp.bfloat16
PARAMS = pltpu.CompilerParams(vmem_limit_bytes=12 * 1024 * 1024)
ALONE = pltpu.CompilerParams(vmem_limit_bytes=63 * 1024 * 1024)


def lane_index(shape):
    return lax.broadcasted_iota(jnp.int32, shape, len(shape) - 1)


def dot(left, right, dims=(((1,), (0,)), ((), ()))):
    return lax.dot_general(left, right, dims, preferred_element_type=F32)


def dense_call(body, out_shape, args, scratch=()):
    return pl.pallas_call(
        body,
        out_shape=out_shape,
        in_specs=[pl.BlockSpec(memory_space=pltpu.VMEM)] * len(args),
        scratch_shapes=list(scratch),
        compiler_params=PARAMS,
    )(*args)


def copies(sources, targets, sems):
    return [
        pltpu.make_async_copy(source, target, sems.at[index])
        for index, (source, target) in enumerate(zip(sources, targets))
    ]


def load(sources, targets, sems):
    started = copies(sources, targets, sems)
    for copy in started:
        copy.start()
    for copy in started:
        copy.wait()


WIRE = LANES + HALF


def pack_body(per_owner, feat_hbm, ends_hbm, list_hbm, out_ref, rows_ref, *refs):
    wide_ref, feat_ref, ends_ref, list_ref, sems = refs
    load((feat_hbm, ends_hbm, list_hbm), (feat_ref, ends_ref, list_ref), sems)
    rest = feat_ref.shape[0] - LANES
    hops = rows_ref.shape[0]
    slot_of = lax.broadcasted_iota(jnp.int32, (LANES, LANES), 0)
    diagonal = slot_of == lane_index((LANES, LANES))
    ends = ends_ref[...]
    found = [jnp.zeros((LANES, LANES), F32) for _ in range(2)]
    for block in range(list_ref.shape[1] // LANES):
        named = list_ref[0:1, block * LANES : (block + 1) * LANES].astype(F32)
        turn = block // hops
        rows_ref[block % hops, turn : turn + 1, :] = named
        named = jnp.sum(jnp.where(diagonal, named, 0.0), axis=1, keepdims=True)
        for side in range(2):
            hit = ends[side : side + 1, :] == slot_of + block * LANES
            found[side] = found[side] + jnp.where(hit, named, 0.0)
    wide_ref[...] = jnp.zeros_like(wide_ref)
    wide_ref[0:rest, :] = feat_ref[LANES:, :].astype(F32)
    wide_ref[rest : rest + 1, :] = jnp.ones((1, LANES), F32)
    for side in range(2):
        spot = rest + 1 + 2 * side
        wide_ref[spot : spot + 1, :] = (ends[side : side + 1, :] // per_owner).astype(F32)
        wide_ref[spot + 1 : spot + 2, :] = jnp.sum(found[side], axis=0, keepdims=True)
    out_ref[0:LANES, :] = feat_ref[0:LANES, :]
    out_ref[LANES:, :] = wide_ref[...].astype(BF16)


def sums_body(rest, nodes, turn_ref, got_ref, list_hbm, out_ref, list_ref, sem):
    copy = pltpu.make_async_copy(list_hbm, list_ref, sem)
    copy.start()
    turns = got_ref.shape[0]
    peers = out_ref.shape[0]
    hops = list_ref.shape[0]
    span = peers * nodes
    base = turn_ref[0] * span
    node_of = lax.broadcasted_iota(jnp.int32, (span, 2 * LANES), 0)
    total = jnp.zeros((span, 2 * LANES), F32)

    def keys(part, side):
        spot = rest + 1 + 2 * side
        rows = got_ref[part, LANES:, :].astype(F32)
        key = rows[spot : spot + 1, :] * nodes + rows[spot + 1 : spot + 2, :]
        return key.astype(jnp.int32) - base

    for part in range(0, turns, 2):
        hits = jnp.zeros((span, 2 * LANES), F32)
        for side in range(2):
            key = jnp.concatenate([keys(part, side), keys(part + 1, side)], axis=1)
            hits = hits + jnp.where(node_of == key, 1.0, 0.0)
        feats = []
        for source in (part, part + 1):
            tail = got_ref[source, LANES:, :]
            feats.append(jnp.concatenate([got_ref[source, 0:LANES, :], tail, tail], axis=0))
        total = total + dot(hits.astype(BF16), jnp.concatenate(feats, axis=1), NT)
    cut = nodes // 2
    lane = lane_index((cut, LANES))
    low_lane = lane < HALF
    spot = jnp.where(low_lane, lane, lane - HALF)
    copy.wait()
    for peer in range(peers):
        mine = total[peer * nodes : (peer + 1) * nodes]
        tail = jnp.where(low_lane, mine[:cut, LANES:], mine[cut:, LANES:])
        high = jnp.floor(tail * (1.0 / LANES))
        tail = jnp.where(spot == rest, tail - high * LANES, tail)
        tail = jnp.where(spot == rest + 1, pltpu.roll(high, 1, 1), tail)
        out_ref[peer, 0:LANES, :] = mine[:, :LANES].astype(BF16)
        out_ref[peer, LANES:WIRE, :] = tail.astype(BF16)
        named = list_ref[peer // (peers // hops)]
        out_ref[peer, WIRE:, :] = jnp.concatenate([named, named], axis=0).astype(BF16)


def mean_body(rest, nodes, got_ref, out_ref):
    total = got_ref[0, 0:WIRE, :].astype(F32)
    for column in range(1, got_ref.shape[0]):
        total = total + got_ref[column, 0:WIRE, :].astype(F32)
    cut = nodes // 2
    head, tail = total[:nodes], total[nodes:]

    def count(start):
        spot = start + rest
        return tail[:, spot : spot + 1] + LANES * tail[:, spot + 1 : spot + 2]

    low, high = count(0), count(HALF)
    low_safe, high_safe = jnp.maximum(low, 1.0), jnp.maximum(high, 1.0)
    head = jnp.concatenate([head[:cut] / low_safe, head[cut:] / high_safe], axis=0)
    lane = lane_index((cut, LANES))
    low_lane = lane < HALF
    spot = jnp.where(low_lane, lane, lane - HALF)
    touched = jnp.where(jnp.where(low_lane, low, high) > 0.5, 1.0, 0.0)
    tail = tail / jnp.where(low_lane, low_safe, high_safe)
    tail = jnp.where(spot < rest, tail, jnp.where(spot == rest, touched, 0.0))
    for part in range(out_ref.shape[0]):
        out_ref[part, 0:nodes, :] = head.astype(BF16)
        out_ref[part, nodes:, :] = tail.astype(BF16)


def pick_body(columns, column_ref, got_ref, out_ref):
    turns, asked, nodes = out_ref.shape
    peers = got_ref.shape[0]
    per_owner = asked // peers
    shift = lax.rem((columns - column_ref[0]) * per_owner, LANES)
    upright = lax.broadcasted_iota(jnp.int32, (per_owner, LANES), 0) == lane_index((per_owner, LANES))
    node_of = lane_index((per_owner, nodes))
    for peer in range(peers):
        named = pltpu.roll(got_ref[peer, WIRE:, :].astype(F32), shift, 1)
        for turn in range(turns):
            row = jnp.where(upright, named[turn : turn + 1, :], 0.0)
            row = jnp.sum(row, axis=1, keepdims=True).astype(jnp.int32)
            hits = jnp.where(row == node_of, 1.0, 0.0).astype(BF16)
            out_ref[turn, peer * per_owner : (peer + 1) * per_owner, :] = hits


def gates(rest, head, tail, head_w_ref, low_w_ref, high_w_ref, gate_ref, bias_ref):
    width = head_w_ref.shape[1]
    message = dot(head, head_w_ref[...]) + jnp.concatenate(
        [dot(tail, low_w_ref[...]), dot(tail, high_w_ref[...])], axis=0
    )
    touched = jnp.concatenate(
        [
            tail[:, rest : rest + 1].astype(F32),
            tail[:, HALF + rest : HALF + rest + 1].astype(F32),
        ],
        axis=0,
    )
    gate = dot(message.astype(BF16), gate_ref[...]) + bias_ref[...]
    update = jax.nn.sigmoid(gate[:, :width]) * jnp.where(touched > 0.5, 1.0, 0.0)
    return 1.0 - update, update * jnp.tanh(gate[:, width:])


def advance(rest, section, mean_ref, batches, memory_ref, weights):
    nodes = memory_ref.shape[0]
    state = memory_ref[...]
    for batch in range(batches):
        head, tail = mean_ref[batch, 0:nodes, :], mean_ref[batch, nodes:, :]
        decay, inject = gates(rest, head, tail, *weights)
        state = jnp.where(section > batch, decay * state + inject, state)
    return state


def before_body(rest, section_ref, mean_ref, memory_ref, *refs):
    weights, out_ref = refs[:-1], refs[-1]
    batches = mean_ref.shape[0] - 1
    before = advance(rest, section_ref[0], mean_ref, batches, memory_ref, weights)
    out_ref[...] = before.astype(BF16)


def rows_body(pick_ref, table_ref, out_ref):
    turns, asked, nodes = pick_ref.shape
    peers, _, width = out_ref.shape
    per_owner = asked // peers
    for turn in range(turns):
        rows = dot(pick_ref[turn], table_ref[turn]).astype(BF16)
        spot = slice(turn * per_owner, (turn + 1) * per_owner)
        out_ref[:, spot, :] = rows.reshape(peers, per_owner, width)


def memory_body(rest, section_ref, mean_ref, memory_ref, *refs):
    weights, out_ref = refs[:-1], refs[-1]
    out_ref[...] = advance(rest, section_ref[0] + 1, mean_ref, mean_ref.shape[0], memory_ref, weights)


def event_body(*refs):
    sources, (scores_ref, grads_ref), targets = refs[:9], refs[9:11], refs[11:20]
    feat_ref, sems = refs[20:]
    rows_ref, ends_ref, near_ref, early_ref, late_ref = targets[:5]
    cot_ref, attn_ref, pred_ref, pred_out_ref = targets[5:]
    started = copies(sources, targets, sems)
    _, ends_copy, near_copy, early_copy, late_copy = started[:5]
    cot_copy, attn_copy, pred_copy, out_copy = started[5:]
    piece = rows_ref.shape[0] // 2
    rows_copies = [
        pltpu.make_async_copy(
            sources[0].at[pl.ds(part * piece, piece)],
            rows_ref.at[pl.ds(part * piece, piece)],
            sems.at[len(sources) * part],
        )
        for part in range(2)
    ]
    for copy in (ends_copy, *rows_copies, near_copy):
        copy.start()
    ends_copy.wait()
    slots, width = rows_ref.shape
    events = ends_ref.shape[1]
    pair = 2 * events
    near_count = near_ref.shape[0] // 2
    head_dim = width // HEADS
    diagonal = lax.broadcasted_iota(jnp.int32, (events, events), 0) == lane_index((events, events))

    def upright(index):
        index = jnp.where(diagonal, index.astype(F32), 0.0)
        return jnp.sum(index, axis=1, keepdims=True).astype(jnp.int32)

    def fetch(source, target):
        index = jnp.concatenate([upright(source), upright(target)], axis=0)
        lanes = lane_index((pair, slots))
        return dot(jnp.where(index == lanes, 1.0, 0.0).astype(BF16), rows_ref[...])

    spots = jnp.concatenate([upright(ends_ref[0:1, :]), upright(ends_ref[1:2, :])], axis=0)
    own = jnp.zeros((pair, width), F32)
    for part in range(2):
        rows_copies[part].wait()
        hits = jnp.where(spots == lane_index((pair, piece)) + part * piece, 1.0, 0.0)
        own = own + dot(hits.astype(BF16), rows_ref[part * piece : (part + 1) * piece, :])
    for copy in (early_copy, attn_copy, late_copy, cot_copy, out_copy, pred_copy):
        copy.start()
    near_copy.wait()
    for near in range(near_count):
        spot = slice(near * pair, (near + 1) * pair)
        other = near_count + near
        feat = fetch(near_ref[near : near + 1, :], near_ref[other : other + 1, :])
        half = near_count // 2
        if near == 0:
            early_copy.wait()
        if near == half:
            late_copy.wait()
        cos_ref = early_ref if near < half else late_ref
        cosines = cos_ref[near % half * pair : (near % half + 1) * pair, :]
        feat_ref[spot, :] = (feat + cosines).astype(BF16)
    attn_copy.wait()
    query = dot(own.astype(BF16), attn_ref[0]) * (1.0 / math.sqrt(head_dim))
    keys = dot(feat_ref[...], attn_ref[1])
    logits = [[] for _ in range(HEADS)]
    for near in range(near_count):
        match = query * keys[near * pair : (near + 1) * pair]
        for head in range(HEADS):
            part = match[:, head * head_dim : (head + 1) * head_dim]
            logits[head].append(jnp.sum(part, axis=1, keepdims=True))
    values = dot(feat_ref[...], attn_ref[2])
    mixed = []
    for head in range(HEADS):
        top = logits[head][0]
        for near in range(1, near_count):
            top = jnp.maximum(top, logits[head][near])
        powers = [jnp.exp(logit - top) for logit in logits[head]]
        total = powers[0]
        for near in range(1, near_count):
            total = total + powers[near]
        part = jnp.zeros((pair, head_dim), F32)
        for near in range(near_count):
            value = values[near * pair : (near + 1) * pair, head * head_dim : (head + 1) * head_dim]
            part = part + (powers[near] / total) * value
        mixed.append(part)
    mixed = jnp.concatenate(mixed, axis=1).astype(BF16)
    state = (own + dot(mixed, attn_ref[3])).astype(BF16)
    source, target = state[:events], state[events:]
    cot_copy.wait()
    out_copy.wait()
    pred_copy.wait()
    pre = dot(source, pred_ref[0]) + dot(target, pred_ref[1])
    gate = jax.nn.sigmoid(pre)
    pred_out = pred_out_ref[...]
    column = jnp.sum(pre * gate * pred_out, axis=1, keepdims=True)
    scores_ref[...] = jnp.sum(jnp.where(diagonal, column, 0.0), axis=0, keepdims=True)
    cot = jnp.sum(jnp.where(diagonal, cot_ref[...], 0.0), axis=1, keepdims=True)
    slope = (cot * pred_out * (gate * (1.0 + pre * (1.0 - gate)))).astype(BF16)
    back = jnp.concatenate([dot(slope, pred_ref[0], NT), dot(slope, pred_ref[1], NT)], axis=0)
    halves = width // LANES
    for index, (left, right) in enumerate(
        ((mixed, back.astype(BF16)), (source, slope), (target, slope))
    ):
        grad = dot(left, right, TN).astype(BF16)
        for half in range(halves):
            start = (index * halves + half) * width
            grads_ref[start : start + width, :] = grad[:, half * LANES : (half + 1) * LANES]


def grads_body(whole_ref, first_ref, rest_ref):
    width = first_ref.shape[0]
    halves = width // LANES
    whole = whole_ref[...].astype(F32).reshape(3 * halves * width, LANES)
    for half in range(halves):
        spot = slice(half * LANES, (half + 1) * LANES)
        first_ref[:, spot] = whole[half * width : (half + 1) * width]
        for part in range(2):
            start = ((part + 1) * halves + half) * width
            rest_ref[part, :, spot] = whole[start : start + width]


def exchange(value, axis, groups=None):
    return lax.all_to_all(
        value, axis, split_axis=0, concat_axis=0, tiled=True, axis_index_groups=groups
    )


def sum_everywhere(grads, line, peers, width):
    sections = lax.axis_size("tm")
    turns = len(line[0])
    near = [
        [(section * turns + turn) * peers + peer for section in range(sections) for peer in range(peers)]
        for turn in range(turns)
    ]
    group = len(near[0])
    own = grads.shape[0] // group
    pieces = exchange(grads.reshape(group, own, LANES), ("tm", "dp"), near)
    mine = jnp.sum(pieces.astype(F32), axis=0).astype(BF16)
    pieces = exchange(jnp.broadcast_to(mine[None], (turns, own, LANES)), "dp", line)
    mine = jnp.sum(pieces.astype(F32), axis=0).astype(BF16)
    whole = exchange(jnp.broadcast_to(mine[None], (group, own, LANES)), ("tm", "dp"), near)
    return dense_call(
        grads_body,
        (
            jax.ShapeDtypeStruct((width, width), F32),
            jax.ShapeDtypeStruct((2, width, width), F32),
        ),
        (whole,),
    )


def per_device(
    edge_feat,
    endpoint_slots,
    neighbor_slots,
    neighbor_gap,
    score_grad,
    node_list,
    memory0,
    msg_weight,
    gate_weight,
    gate_bias,
    omega,
    attn_weights,
    pred_weights,
    pred_out,
):
    groups = lax.axis_size("dp")
    batches = lax.axis_size("tm")
    nodes, width = memory0.shape
    list_len = node_list.shape[2]
    per_owner = list_len // groups
    features = edge_feat.shape[2]
    rest = features - LANES
    events = endpoint_slots.shape[2]
    near_count = neighbor_slots.shape[1] // 2
    columns = 4
    hops = 2
    rings = groups // columns
    turns = rings // hops
    peers = hops * columns
    line = [
        [(turn * hops + hop) * columns + column for turn in range(turns)]
        for column in range(columns)
        for hop in range(hops)
    ]
    across = [[turn * peers + peer for peer in range(peers)] for turn in range(turns)]
    place = lax.axis_index("dp").astype(jnp.int32)
    sent, named = pl.pallas_call(
        lambda *refs: pack_body(per_owner, *refs),
        out_shape=(
            jax.ShapeDtypeStruct((WIRE, LANES), BF16),
            jax.ShapeDtypeStruct((hops, turns, LANES), F32),
        ),
        in_specs=[pl.BlockSpec(memory_space=pltpu.HBM)] * 3,
        scratch_shapes=[
            pltpu.VMEM((HALF, LANES), F32),
            pltpu.VMEM((features, events), BF16),
            pltpu.VMEM((2, events), jnp.int32),
            pltpu.VMEM((1, list_len), jnp.int32),
            pltpu.SemaphoreType.DMA((3,)),
        ],
        compiler_params=ALONE,
    )(jnp.swapaxes(edge_feat[0], 0, 1), endpoint_slots[0], node_list[0])
    got = lax.all_gather(sent, "dp", axis=0, tiled=True, axis_index_groups=line)
    in_smem, in_vmem = pl.BlockSpec(memory_space=pltpu.SMEM), pl.BlockSpec(memory_space=pltpu.VMEM)
    sums = pl.pallas_call(
        lambda *refs: sums_body(rest, nodes, *refs),
        out_shape=jax.ShapeDtypeStruct((peers, WIRE + 2 * turns, LANES), BF16),
        in_specs=[in_smem, in_vmem, pl.BlockSpec(memory_space=pltpu.HBM)],
        scratch_shapes=[pltpu.VMEM((hops, turns, LANES), F32), pltpu.SemaphoreType.DMA],
        compiler_params=PARAMS,
    )(
        (place // peers)[None],
        got.reshape(turns, WIRE, LANES),
        pltpu.with_memory_space_constraint(named, pltpu.HBM),
    )
    got = exchange(sums, "dp", across)
    picks = pl.pallas_call(
        lambda *refs: pick_body(columns, *refs),
        out_shape=jax.ShapeDtypeStruct((turns, peers * per_owner, nodes), BF16),
        in_specs=[in_smem, in_vmem],
        compiler_params=PARAMS,
    )((place % columns)[None], got)
    pairs = 2 * near_count * events

    def by_neighbour(value):
        return jnp.swapaxes(value[0].reshape(2, near_count, events), 0, 1).reshape(pairs, 1)

    gaps = by_neighbour(neighbor_gap).astype(F32)
    cut = pairs // 2
    early = jnp.cos(gaps[:cut] * omega[None, :])
    means = dense_call(
        lambda *refs: mean_body(rest, nodes, *refs),
        jax.ShapeDtypeStruct((batches, nodes + nodes // 2, LANES), BF16),
        (got,),
    )
    def arrived(slot):
        owner, spot = slot // per_owner, slot % per_owner
        turn, peer = owner // peers, owner % peers
        return (peer * turns + turn) * per_owner + spot

    means, picks, early, end_spots, near_spots = lax.optimization_barrier(
        (
            exchange(means, "tm"),
            picks,
            early,
            arrived(endpoint_slots[0]),
            arrived(neighbor_slots[0]),
        )
    )
    tail_w = jnp.pad(msg_weight[LANES:], ((0, HALF - rest), (0, 0)))
    section = lax.axis_index("tm").astype(jnp.int32)
    weights = (
        msg_weight[:LANES],
        jnp.pad(tail_w, ((0, HALF), (0, 0))),
        jnp.pad(tail_w, ((HALF, 0), (0, 0))),
        gate_weight,
        gate_bias[None],
    )

    def section_call(body, out_shape, args):
        return pl.pallas_call(
            lambda *refs: body(rest, *refs),
            out_shape=out_shape,
            in_specs=[pl.BlockSpec(memory_space=pltpu.SMEM)]
            + [pl.BlockSpec(memory_space=pltpu.VMEM)] * (len(args) + len(weights)),
            compiler_params=PARAMS,
        )(section[None], *args, *weights)

    before = section_call(
        before_body,
        jax.ShapeDtypeStruct((nodes, width), BF16),
        (means, memory0),
    )
    table = lax.all_gather(before, "dp", axis=0, tiled=True, axis_index_groups=line)
    table = table.reshape(turns, nodes, width)
    new_memory = section_call(
        memory_body, jax.ShapeDtypeStruct((nodes, width), F32), (means, memory0)
    )
    rows = dense_call(
        rows_body,
        jax.ShapeDtypeStruct((peers, turns * per_owner, width), BF16),
        (picks, table),
    )
    rows, omega_late = lax.optimization_barrier((rows, omega))
    slot_rows = exchange(rows, "dp", across).reshape(list_len, width)
    late = jnp.cos(gaps[cut:] * omega_late[None, :])
    late, new_memory = lax.optimization_barrier((late, new_memory))

    inputs = (
        slot_rows,
        end_spots,
        near_spots,
        early,
        late,
        score_grad,
        attn_weights,
        pred_weights,
        pred_out[None],
    )
    scores, grads = pl.pallas_call(
        event_body,
        out_shape=(
            jax.ShapeDtypeStruct((1, events), F32),
            jax.ShapeDtypeStruct((3 * width * width // LANES, LANES), BF16),
        ),
        in_specs=[pl.BlockSpec(memory_space=pltpu.HBM)] * len(inputs),
        scratch_shapes=[pltpu.VMEM(value.shape, value.dtype) for value in inputs]
        + [pltpu.VMEM((pairs, width), BF16), pltpu.SemaphoreType.DMA((len(inputs) + 1,))],
        compiler_params=ALONE,
    )(*inputs)
    grad_out, grad_pair = sum_everywhere(grads, line, peers, width)
    return (scores, new_memory[None], grad_out, grad_pair)


def solution(mesh):
    in_specs = (
        P("tm", "dp", None),
        P("tm", None, "dp"),
        P("tm", None, "dp"),
        P("tm", None, "dp"),
        P("tm", "dp"),
        P("tm", "dp", None),
        P("dp", None),
        P(),
        P(),
        P(),
        P(),
        P(),
        P(),
        P(),
    )
    out_specs = (P("tm", "dp"), P("tm", "dp", None), P(), P())
    return jax.shard_map(
        per_device, mesh=mesh, in_specs=in_specs, out_specs=out_specs, check_vma=False
    )
```
